128 devices in a mesh: occ: 4 (over y_lo, core), vir: 32 (over z, x, y_hi).
Axes of the slice: x: 4, y: 4 (y_hi: 2, y_lo: 2; y = y_hi * 2 + y_lo), z: 4, core: 2. Of those that a mesh axis runs over, the one named last changes fastest.
Arguments:
- amplitudes: bfloat16 [8, 1024, 1024], P('occ', 'vir'), may hold values from -6 to 6
- factors: bfloat16 [96, 1024, 1024], P('vir'), may hold values from -0.0625 to 0.0625
- occ_energy: float32 [100], replicated, may hold values from -2 to -0.3
- vir_energy: float32 [1024], replicated, may hold values from 0.3 to 4
- occ_irrep: int32 [100], replicated, may hold values from 0 to 7
- vir_irrep: int32 [1024], replicated, may hold values from 0 to 7
- pair_orbitals: int32 [8, 2], replicated, may hold values from 0 to 99, as said below
Outputs:
- update: float32 [8, 1024, 1024], P('occ', 'vir')
The draws below stay inside these ranges and needn't reach their ends.
Inputs may be any that keep to these rules, and one draw needn't show every extreme that they name: `pair_orbitals`: pair p + 4 is pair p with i and j swapped; the orbitals named by the first 4 pairs are all distinct.
All inputs are finite; a program needn't handle non-finite values.
Results may differ from the reference program's by a relative error of at most 0.0029.
Values may be sent and summed in bfloat16 or wider, within the bound.
A program may use at most 128 MiB of HBM per device.

```python
import jax
import jax.numpy as jnp
from jax import lax

V = 1024
NOCC = 100
PAIRS = 8
NAUX = 96


def draw_pair_orbitals(key, part):
    inner = 1 + jax.random.permutation(jax.random.fold_in(key, 11), NOCC - 2)
    ends = jnp.array([0, NOCC - 1], dtype=jnp.int32)
    chosen = jnp.concatenate([ends, inner[:PAIRS - 2].astype(jnp.int32)], axis=0)
    mixing = jax.random.permutation(jax.random.fold_in(key, 23), PAIRS)
    chosen = chosen[mixing]
    half_pairs = PAIRS // 2
    first_orb = chosen[:half_pairs]
    second_orb = chosen[half_pairs:PAIRS]
    upper = jnp.stack([first_orb, second_orb], axis=1)
    lower = jnp.stack([second_orb, first_orb], axis=1)
    return jnp.concatenate([upper, lower], axis=0).astype(jnp.int32)


def plant(entries, own_key, least, high):
    longest = entries.shape.index(max(entries.shape))
    spots = []
    for shift in (0, 1):
        where = [jax.random.randint(jax.random.fold_in(own_key, axis), (), 0, length) for axis, length in enumerate(entries.shape)]
        where[longest] = (where[longest] + shift) % entries.shape[longest]
        spots.append(tuple(where))
    return entries.at[spots[0]].set(least).at[spots[1]].set(high)


def levels(rng, shape, cuts, smallest, high):
    loudness = 1.0
    for position, parts in cuts:
        draws = jax.random.uniform(jax.random.fold_in(jax.random.fold_in(rng, 6), position), (parts,), jnp.float32, smallest / len(cuts), high / len(cuts))
        loudness = loudness * jnp.repeat(jnp.exp(draws), shape[position] // parts).reshape((-1,) + (1,) * (len(shape) - 1 - position))
    return loudness


def centred(rng, shape, deviation, reach, split=(), held_as=jnp.bfloat16):
    values = jax.random.normal(rng, shape, jnp.float32) * deviation
    if len(split) > 0:
        values = levels(rng, shape, split, -0.22, 0.18) * values
    return jnp.clip(values, min=-reach, max=reach).astype(held_as)


def setup_inputs(seed: int = 0) -> dict:
    arg_keys = jax.random.split(jax.random.key(seed), 8)
    return {
        "amplitudes": centred(arg_keys[0], (PAIRS, V, V), 1.0, 6.0, ((0, 4), (1, 32))),
        "factors": centred(arg_keys[1], (NAUX, V, V), (V * 10) ** -0.5, 0.0625, ((0, 32),)),
        "occ_energy": jnp.clip(jax.random.uniform(arg_keys[2], (NOCC,), jnp.float32, -2.0, -0.3), -2.0, -0.3),
        "vir_energy": jnp.clip(jax.random.uniform(arg_keys[3], (V,), jnp.float32, 0.3, 4.0), 0.3, 4.0),
        "occ_irrep": plant(jax.random.randint(arg_keys[4], (NOCC,), 0, 8), jax.random.fold_in(arg_keys[4], 1), 0, 7).astype(jnp.int32),
        "vir_irrep": plant(jax.random.randint(arg_keys[5], (V,), 0, 8), jax.random.fold_in(arg_keys[5], 1), 0, 7).astype(jnp.int32),
        "pair_orbitals": draw_pair_orbitals(jax.random.fold_in(arg_keys[7], 71), 0),
    }


def reference(amplitudes, factors, occ_energy, vir_energy, occ_irrep, vir_irrep, pair_orbitals):
    amp_values = amplitudes.astype(jnp.float32)
    highest = lax.Precision.HIGHEST

    def add_vector(running, factor):
        fac_values = factor.astype(jnp.float32)
        halves = jnp.einsum('pcd,bd->pcb', amp_values, fac_values, precision=highest)
        halves = lax.optimization_barrier(halves.astype(jnp.bfloat16)).astype(jnp.float32)
        ladder = jnp.einsum('ac,pcb->pab', fac_values, halves, precision=highest)
        return running + ladder, None

    summed, _ = lax.scan(add_vector, jnp.zeros((PAIRS, V, V), jnp.float32), factors)
    partner = jnp.transpose(jnp.roll(summed, PAIRS // 2, axis=0), (0, 2, 1))
    first_orb = pair_orbitals[:, 0]
    second_orb = pair_orbitals[:, 1]
    pair_energy = occ_energy[first_orb] + occ_energy[second_orb]
    denominator = vir_energy[None, :, None] + vir_energy[None, None, :] - pair_energy[:, None, None]
    pair_sym = jnp.bitwise_xor(occ_irrep[first_orb], occ_irrep[second_orb])
    combined = jnp.bitwise_xor(jnp.bitwise_xor(pair_sym[:, None, None], vir_irrep[None, :, None]), vir_irrep[None, None, :])
    allowed = combined == 0
    return jnp.where(allowed, (summed + partner) / denominator, jnp.float32(0.0))
```

```python
import jax
import jax.numpy as jnp
from jax import lax
from jax.sharding import PartitionSpec as P


def passed_along(block, axis, distance):
    devices = range(lax.axis_size(axis))
    route = [((i - distance) % len(devices), i) for i in devices]
    return lax.ppermute(block, axis, route)


def per_device(amplitudes, factors, occ_energy, vir_energy, occ_irrep, vir_irrep, pair_orbitals):
    local_pairs = amplitudes.shape[0]
    row_count = amplitudes.shape[1]
    occ_total = occ_energy.shape[0]
    occ_devices = lax.axis_size("occ")
    vir_devices = lax.axis_size("vir")
    occ_index = lax.axis_index("occ")
    vir_index = lax.axis_index("vir")
    lower_half = occ_index < occ_devices // 2

    outgoing = jnp.where(lower_half, amplitudes[1], amplitudes[0])
    incoming = passed_along(outgoing, "occ", occ_devices // 2)
    first = jnp.where(lower_half, amplitudes[0], incoming)
    second = jnp.where(lower_half, incoming, amplitudes[1])
    couple = jnp.stack([first, second], axis=0)
    gathered = lax.all_gather(couple, "vir", axis=1, tiled=True)

    def half_product(factor):
        product = jnp.einsum("pcd,bd->pbc", gathered, factor, preferred_element_type=jnp.float32)
        return product.astype(jnp.bfloat16)

    halves = lax.map(half_product, factors)
    direct = jnp.einsum("qac,qbc->ab", factors, halves[:, 0], preferred_element_type=jnp.float32)
    turned_term = jnp.einsum("qac,qbc->ab", halves[:, 1], factors, preferred_element_type=jnp.float32)
    combined = direct + turned_term
    own_rows = lax.psum_scatter(combined, "vir", scatter_dimension=0, tiled=True)
    cols = lax.all_to_all(own_rows, "vir", split_axis=1, concat_axis=0, tiled=True)
    own_cols = jnp.transpose(cols, (1, 0))
    outgoing_block = jnp.where(lower_half, own_cols, own_rows)
    incoming_block = passed_along(outgoing_block, "occ", occ_devices // 2)
    first_out = jnp.where(lower_half, own_rows, incoming_block)
    second_out = jnp.where(lower_half, incoming_block, own_cols)
    summed_pair = jnp.stack([first_out, second_out], axis=0)

    pair_ids = lax.dynamic_slice_in_dim(pair_orbitals, occ_index * local_pairs, local_pairs, 0)
    row_start = vir_index * row_count
    energy_rows = lax.dynamic_slice_in_dim(vir_energy, row_start, row_count, 0)
    irrep_rows = lax.dynamic_slice_in_dim(vir_irrep, row_start, row_count, 0)
    positions = jnp.arange(occ_total, dtype=jnp.int32)
    first_hot = positions[None, :] == pair_ids[:, 0:1]
    second_hot = positions[None, :] == pair_ids[:, 1:2]
    pair_energy = jnp.sum(jnp.where(first_hot, occ_energy[None, :], 0.0), axis=1) + jnp.sum(
        jnp.where(second_hot, occ_energy[None, :], 0.0), axis=1
    )
    first_irrep = jnp.sum(jnp.where(first_hot, occ_irrep[None, :], 0), axis=1)
    second_irrep = jnp.sum(jnp.where(second_hot, occ_irrep[None, :], 0), axis=1)
    pair_sym = jnp.bitwise_xor(first_irrep, second_irrep)
    combined_sym = jnp.bitwise_xor(
        jnp.bitwise_xor(pair_sym[:, None, None], irrep_rows[None, :, None]),
        vir_irrep[None, None, :],
    )
    allowed = combined_sym == 0
    denominator = (
        energy_rows[None, :, None] + vir_energy[None, None, :] - pair_energy[:, None, None]
    )
    return jnp.where(allowed, summed_pair / denominator, jnp.float32(0.0))


def solution(mesh):
    return jax.shard_map(
        per_device,
        mesh=mesh,
        in_specs=(P("occ", "vir", None), P("vir", None, None), P(), P(), P(), P(), P()),
        out_specs=P("occ", "vir", None),
        check_vma=False,
    )
```

```python
import jax
import jax.numpy as jnp
from jax import lax
from jax.sharding import PartitionSpec as P


def passed_along(block, axis, distance):
    devices = range(lax.axis_size(axis))
    route = [((i - distance) % len(devices), i) for i in devices]
    return lax.ppermute(block, axis, route)


def per_device(amplitudes, factors, occ_energy, vir_energy, occ_irrep, vir_irrep, pair_orbitals):
    local_pairs = amplitudes.shape[0]
    row_count = amplitudes.shape[1]
    occ_total = occ_energy.shape[0]
    occ_devices = lax.axis_size("occ")
    vir_devices = lax.axis_size("vir")
    occ_index = lax.axis_index("occ")
    vir_index = lax.axis_index("vir")
    lower_half = occ_index < occ_devices // 2

    outgoing = jnp.where(lower_half, amplitudes[1], amplitudes[0])
    incoming = passed_along(outgoing, "occ", occ_devices // 2)
    first = jnp.where(lower_half, amplitudes[0], incoming)
    second = jnp.where(lower_half, incoming, amplitudes[1])
    couple = jnp.stack([first, second], axis=0)
    spread = jnp.broadcast_to(couple[None], (vir_devices,) + couple.shape)
    pieces = lax.all_to_all(spread, "vir", split_axis=0, concat_axis=0, tiled=True)
    gathered = jnp.transpose(pieces, (1, 0, 2, 3)).reshape(2, vir_devices * row_count, couple.shape[-1])

    def half_product(factor):
        product = jnp.einsum("pcd,bd->pbc", gathered, factor, preferred_element_type=jnp.float32)
        return product.astype(jnp.bfloat16)

    halves = lax.map(half_product, factors)
    direct = jnp.einsum("qac,qbc->ab", factors, halves[:, 0], preferred_element_type=jnp.float32)
    turned_term = jnp.einsum("qac,qbc->ab", halves[:, 1], factors, preferred_element_type=jnp.float32)
    combined = direct + turned_term
    blocks = combined.reshape(vir_devices, row_count, combined.shape[-1])
    arrived = lax.all_to_all(blocks, "vir", split_axis=0, concat_axis=0, tiled=True)
    own_rows = jnp.sum(arrived, axis=0)
    cols = lax.all_to_all(own_rows, "vir", split_axis=1, concat_axis=0, tiled=True)
    own_cols = jnp.transpose(cols, (1, 0))
    outgoing_block = jnp.where(lower_half, own_cols, own_rows)
    incoming_block = passed_along(outgoing_block, "occ", occ_devices // 2)
    first_out = jnp.where(lower_half, own_rows, incoming_block)
    second_out = jnp.where(lower_half, incoming_block, own_cols)
    summed_pair = jnp.stack([first_out, second_out], axis=0)

    pair_ids = lax.dynamic_slice_in_dim(pair_orbitals, occ_index * local_pairs, local_pairs, 0)
    row_start = vir_index * row_count
    energy_rows = lax.dynamic_slice_in_dim(vir_energy, row_start, row_count, 0)
    irrep_rows = lax.dynamic_slice_in_dim(vir_irrep, row_start, row_count, 0)
    positions = jnp.arange(occ_total, dtype=jnp.int32)
    first_hot = positions[None, :] == pair_ids[:, 0:1]
    second_hot = positions[None, :] == pair_ids[:, 1:2]
    pair_energy = jnp.sum(jnp.where(first_hot, occ_energy[None, :], 0.0), axis=1) + jnp.sum(
        jnp.where(second_hot, occ_energy[None, :], 0.0), axis=1
    )
    first_irrep = jnp.sum(jnp.where(first_hot, occ_irrep[None, :], 0), axis=1)
    second_irrep = jnp.sum(jnp.where(second_hot, occ_irrep[None, :], 0), axis=1)
    pair_sym = jnp.bitwise_xor(first_irrep, second_irrep)
    combined_sym = jnp.bitwise_xor(
        jnp.bitwise_xor(pair_sym[:, None, None], irrep_rows[None, :, None]),
        vir_irrep[None, None, :],
    )
    allowed = combined_sym == 0
    denominator = (
        energy_rows[None, :, None] + vir_energy[None, None, :] - pair_energy[:, None, None]
    )
    return jnp.where(allowed, summed_pair / denominator, jnp.float32(0.0))


def solution(mesh):
    return jax.shard_map(
        per_device,
        mesh=mesh,
        in_specs=(P("occ", "vir", None), P("vir", None, None), P(), P(), P(), P(), P()),
        out_specs=P("occ", "vir", None),
        check_vma=False,
    )
```

```python
import jax
import jax.numpy as jnp
from jax import lax
from jax.sharding import PartitionSpec as P


def passed_along(block, axis, distance):
    devices = range(lax.axis_size(axis))
    route = [((i - distance) % len(devices), i) for i in devices]
    return lax.ppermute(block, axis, route)


def per_device(amplitudes, factors, occ_energy, vir_energy, occ_irrep, vir_irrep, pair_orbitals):
    local_pairs = amplitudes.shape[0]
    row_count = amplitudes.shape[1]
    occ_total = occ_energy.shape[0]
    occ_devices = lax.axis_size("occ")
    vir_devices = lax.axis_size("vir")
    occ_index = lax.axis_index("occ")
    vir_index = lax.axis_index("vir")
    lower_half = occ_index < occ_devices // 2

    outgoing = jnp.where(lower_half, amplitudes[1], amplitudes[0])
    incoming = passed_along(outgoing, "occ", occ_devices // 2)
    first = jnp.where(lower_half, amplitudes[0], incoming)
    second = jnp.where(lower_half, incoming, amplitudes[1])
    def gather_rows(block):
        spread = jnp.broadcast_to(block[None], (vir_devices,) + block.shape)
        pieces = lax.all_to_all(spread, "vir", split_axis=0, concat_axis=0, tiled=True)
        return pieces.reshape(vir_devices * row_count, block.shape[-1])

    def half_products(rows):
        def half_product(factor):
            product = jnp.einsum("cd,bd->bc", rows, factor, preferred_element_type=jnp.float32)
            return product.astype(jnp.bfloat16)

        return lax.map(half_product, factors)

    halves_first = half_products(gather_rows(first))
    halves_second = half_products(gather_rows(second))
    width = factors.shape[1]
    chunks = 4
    chunk = width // chunks
    own_parts = []
    for part in range(chunks):
        cut = slice(part * chunk, (part + 1) * chunk)
        direct = jnp.einsum("qac,qbc->ab", factors, halves_first[:, cut], preferred_element_type=jnp.float32)
        turned_term = jnp.einsum(
            "qac,qbc->ab", halves_second, factors[:, cut], preferred_element_type=jnp.float32
        )
        combined = direct + turned_term
        blocks = combined.reshape(vir_devices, row_count, chunk)
        arrived = lax.all_to_all(blocks, "vir", split_axis=0, concat_axis=0, tiled=True)
        own_parts.append(jnp.sum(arrived, axis=0))
    own_rows = jnp.concatenate(own_parts, axis=1)
    cols = lax.all_to_all(own_rows, "vir", split_axis=1, concat_axis=0, tiled=True)
    own_cols = jnp.transpose(cols, (1, 0))
    outgoing_block = jnp.where(lower_half, own_cols, own_rows)
    incoming_block = passed_along(outgoing_block, "occ", occ_devices // 2)
    first_out = jnp.where(lower_half, own_rows, incoming_block)
    second_out = jnp.where(lower_half, incoming_block, own_cols)
    summed_pair = jnp.stack([first_out, second_out], axis=0)

    pair_ids = lax.dynamic_slice_in_dim(pair_orbitals, occ_index * local_pairs, local_pairs, 0)
    row_start = vir_index * row_count
    energy_rows = lax.dynamic_slice_in_dim(vir_energy, row_start, row_count, 0)
    irrep_rows = lax.dynamic_slice_in_dim(vir_irrep, row_start, row_count, 0)
    positions = jnp.arange(occ_total, dtype=jnp.int32)
    first_hot = positions[None, :] == pair_ids[:, 0:1]
    second_hot = positions[None, :] == pair_ids[:, 1:2]
    pair_energy = jnp.sum(jnp.where(first_hot, occ_energy[None, :], 0.0), axis=1) + jnp.sum(
        jnp.where(second_hot, occ_energy[None, :], 0.0), axis=1
    )
    first_irrep = jnp.sum(jnp.where(first_hot, occ_irrep[None, :], 0), axis=1)
    second_irrep = jnp.sum(jnp.where(second_hot, occ_irrep[None, :], 0), axis=1)
    pair_sym = jnp.bitwise_xor(first_irrep, second_irrep)
    combined_sym = jnp.bitwise_xor(
        jnp.bitwise_xor(pair_sym[:, None, None], irrep_rows[None, :, None]),
        vir_irrep[None, None, :],
    )
    allowed = combined_sym == 0
    denominator = (
        energy_rows[None, :, None] + vir_energy[None, None, :] - pair_energy[:, None, None]
    )
    return jnp.where(allowed, summed_pair / denominator, jnp.float32(0.0))


def solution(mesh):
    return jax.shard_map(
        per_device,
        mesh=mesh,
        in_specs=(P("occ", "vir", None), P("vir", None, None), P(), P(), P(), P(), P()),
        out_specs=P("occ", "vir", None),
        check_vma=False,
    )
```

```python
import functools

import jax
import jax.numpy as jnp
from jax import lax
from jax.sharding import PartitionSpec as P
from jax.experimental import pallas as pl
from jax.experimental.pallas import tpu as pltpu


def passed_along(block, axis, distance):
    devices = range(lax.axis_size(axis))
    route = [((i - distance) % len(devices), i) for i in devices]
    return lax.ppermute(block, axis, route)


def _scatter_kernel(n, c_ref, out_ref, send_sems, recv_sems, local_sem):
    me = lax.axis_index("vir")
    group = lax.axis_index("occ")
    rows = out_ref.shape[1]

    barrier = pltpu.get_barrier_semaphore()

    def greet(k, carry):
        peer = lax.rem(me + k, n)
        pl.semaphore_signal(barrier, inc=1, device_id=(group, peer), device_id_type=pl.DeviceIdType.MESH)
        return carry

    lax.fori_loop(1, n, greet, 0)
    pl.semaphore_wait(barrier, n - 1)

    own = pltpu.make_async_copy(c_ref.at[pl.ds(me * rows, rows)], out_ref.at[me], local_sem)
    own.start()

    def send(k, carry):
        peer = lax.rem(me + k, n)
        pltpu.make_async_remote_copy(
            src_ref=c_ref.at[pl.ds(peer * rows, rows)],
            dst_ref=out_ref.at[me],
            send_sem=send_sems.at[peer],
            recv_sem=recv_sems.at[me],
            device_id=(group, peer),
            device_id_type=pl.DeviceIdType.MESH,
        ).start()
        return carry

    lax.fori_loop(1, n, send, 0)

    def finish(k, carry):
        peer = lax.rem(me + k, n)
        source = lax.rem(me + n - k, n)
        pltpu.make_async_remote_copy(
            src_ref=c_ref.at[pl.ds(peer * rows, rows)],
            dst_ref=out_ref.at[me],
            send_sem=send_sems.at[peer],
            recv_sem=recv_sems.at[me],
            device_id=(group, peer),
            device_id_type=pl.DeviceIdType.MESH,
        ).wait_send()
        pltpu.make_async_remote_copy(
            src_ref=c_ref.at[pl.ds(me * rows, rows)],
            dst_ref=out_ref.at[source],
            send_sem=send_sems.at[source],
            recv_sem=recv_sems.at[source],
            device_id=(group, source),
            device_id_type=pl.DeviceIdType.MESH,
        ).wait_recv()
        return carry

    lax.fori_loop(1, n, finish, 0)
    own.wait()


def reduce_rows(c, occ_axis, vir_axis):
    n = lax.axis_size(vir_axis)
    rows = c.shape[0] // n
    arrived = pl.pallas_call(
        functools.partial(_scatter_kernel, n),
        out_shape=jax.ShapeDtypeStruct((n, rows, c.shape[1]), c.dtype),
        in_specs=[pl.BlockSpec(memory_space=pl.ANY)],
        out_specs=pl.BlockSpec(memory_space=pl.ANY),
        scratch_shapes=[
            pltpu.SemaphoreType.DMA((n,)),
            pltpu.SemaphoreType.DMA((n,)),
            pltpu.SemaphoreType.DMA,
        ],
        compiler_params=pltpu.CompilerParams(collective_id=0, has_side_effects=True),
    )(c)
    return jnp.sum(arrived, axis=0)


def per_device(amplitudes, factors, occ_energy, vir_energy, occ_irrep, vir_irrep, pair_orbitals):
    local_pairs = amplitudes.shape[0]
    row_count = amplitudes.shape[1]
    occ_total = occ_energy.shape[0]
    occ_devices = lax.axis_size("occ")
    vir_devices = lax.axis_size("vir")
    occ_index = lax.axis_index("occ")
    vir_index = lax.axis_index("vir")
    lower_half = occ_index < occ_devices // 2

    outgoing = jnp.where(lower_half, amplitudes[1], amplitudes[0])
    incoming = passed_along(outgoing, "occ", occ_devices // 2)
    first = jnp.where(lower_half, amplitudes[0], incoming)
    second = jnp.where(lower_half, incoming, amplitudes[1])
    couple = jnp.stack([first, second], axis=0)
    spread = jnp.broadcast_to(couple[None], (vir_devices,) + couple.shape)
    pieces = lax.all_to_all(spread, "vir", split_axis=0, concat_axis=0, tiled=True)
    gathered = jnp.transpose(pieces, (1, 0, 2, 3)).reshape(2, vir_devices * row_count, couple.shape[-1])

    def half_product(factor):
        product = jnp.einsum("pcd,bd->pbc", gathered, factor, preferred_element_type=jnp.float32)
        return product.astype(jnp.bfloat16)

    halves = lax.map(half_product, factors)
    direct = jnp.einsum("qac,qbc->ab", factors, halves[:, 0], preferred_element_type=jnp.float32)
    turned_term = jnp.einsum("qac,qbc->ab", halves[:, 1], factors, preferred_element_type=jnp.float32)
    combined = direct + turned_term
    own_rows = reduce_rows(combined, "occ", "vir")
    cols = lax.all_to_all(own_rows, "vir", split_axis=1, concat_axis=0, tiled=True)
    own_cols = jnp.transpose(cols, (1, 0))
    outgoing_block = jnp.where(lower_half, own_cols, own_rows)
    incoming_block = passed_along(outgoing_block, "occ", occ_devices // 2)
    first_out = jnp.where(lower_half, own_rows, incoming_block)
    second_out = jnp.where(lower_half, incoming_block, own_cols)
    summed_pair = jnp.stack([first_out, second_out], axis=0)

    pair_ids = lax.dynamic_slice_in_dim(pair_orbitals, occ_index * local_pairs, local_pairs, 0)
    row_start = vir_index * row_count
    energy_rows = lax.dynamic_slice_in_dim(vir_energy, row_start, row_count, 0)
    irrep_rows = lax.dynamic_slice_in_dim(vir_irrep, row_start, row_count, 0)
    positions = jnp.arange(occ_total, dtype=jnp.int32)
    first_hot = positions[None, :] == pair_ids[:, 0:1]
    second_hot = positions[None, :] == pair_ids[:, 1:2]
    pair_energy = jnp.sum(jnp.where(first_hot, occ_energy[None, :], 0.0), axis=1) + jnp.sum(
        jnp.where(second_hot, occ_energy[None, :], 0.0), axis=1
    )
    first_irrep = jnp.sum(jnp.where(first_hot, occ_irrep[None, :], 0), axis=1)
    second_irrep = jnp.sum(jnp.where(second_hot, occ_irrep[None, :], 0), axis=1)
    pair_sym = jnp.bitwise_xor(first_irrep, second_irrep)
    combined_sym = jnp.bitwise_xor(
        jnp.bitwise_xor(pair_sym[:, None, None], irrep_rows[None, :, None]),
        vir_irrep[None, None, :],
    )
    allowed = combined_sym == 0
    denominator = (
        energy_rows[None, :, None] + vir_energy[None, None, :] - pair_energy[:, None, None]
    )
    return jnp.where(allowed, summed_pair / denominator, jnp.float32(0.0))


def solution(mesh):
    return jax.shard_map(
        per_device,
        mesh=mesh,
        in_specs=(P("occ", "vir", None), P("vir", None, None), P(), P(), P(), P(), P()),
        out_specs=P("occ", "vir", None),
        check_vma=False,
    )
```

```python
import functools

import jax
import jax.numpy as jnp
from jax import lax
from jax.sharding import PartitionSpec as P
from jax.experimental import pallas as pl
from jax.experimental.pallas import tpu as pltpu


def passed_along(block, axis, distance):
    devices = range(lax.axis_size(axis))
    route = [((i - distance) % len(devices), i) for i in devices]
    return lax.ppermute(block, axis, route)


def _exchange_kernel(layout, *refs):
    count = len(layout)
    sources, targets = refs[:count], refs[count:2 * count]
    send_sems, recv_sems = refs[2 * count:3 * count], refs[3 * count:4 * count]
    local_sems = refs[4 * count]
    me = lax.axis_index("vir")
    group = lax.axis_index("occ")

    def peer_of(mine, coord, stride):
        return me + (coord - mine) * stride

    barrier = pltpu.get_barrier_semaphore()
    greetings = 0
    coords = []
    for stride, size, shared in layout:
        mine = lax.rem(lax.div(me, stride), size)
        coords.append(mine)
        for step in range(1, size):
            coord = lax.rem(mine + step, size)
            pl.semaphore_signal(
                barrier, inc=1, device_id=(group, peer_of(mine, coord, stride)),
                device_id_type=pl.DeviceIdType.MESH,
            )
            greetings += 1
    pl.semaphore_wait(barrier, greetings)

    def remote(part, coord, slot):
        stride, size, shared = layout[part]
        mine = coords[part]
        source = sources[part] if shared else sources[part].at[coord]
        return pltpu.make_async_remote_copy(
            src_ref=source,
            dst_ref=targets[part].at[slot],
            send_sem=send_sems[part].at[coord],
            recv_sem=recv_sems[part].at[slot],
            device_id=(group, peer_of(mine, coord, stride)),
            device_id_type=pl.DeviceIdType.MESH,
        )

    locals_ = []
    for part, (stride, size, shared) in enumerate(layout):
        mine = coords[part]
        source = sources[part] if shared else sources[part].at[mine]
        local = pltpu.make_async_copy(source, targets[part].at[mine], local_sems.at[part])
        local.start()
        locals_.append(local)
        for step in range(1, size):
            remote(part, lax.rem(mine + step, size), mine).start()
    for part, (stride, size, shared) in enumerate(layout):
        mine = coords[part]
        for step in range(1, size):
            remote(part, lax.rem(mine + step, size), mine).wait_send()
            origin = lax.rem(mine + size - step, size)
            stride_ = stride
            pltpu.make_async_remote_copy(
                src_ref=sources[part] if shared else sources[part].at[origin],
                dst_ref=targets[part].at[origin],
                send_sem=send_sems[part].at[origin],
                recv_sem=recv_sems[part].at[origin],
                device_id=(group, peer_of(mine, origin, stride_)),
                device_id_type=pl.DeviceIdType.MESH,
            ).wait_recv()
        locals_[part].wait()


def exchange(parts, collective_id):
    layout = tuple((stride, size, shared) for _, stride, size, shared in parts)
    shapes = []
    for array, stride, size, shared in parts:
        block = array.shape if shared else array.shape[1:]
        shapes.append(jax.ShapeDtypeStruct((size,) + tuple(block), array.dtype))
    scratch = [pltpu.SemaphoreType.DMA((size,)) for _, _, size, _ in parts]
    scratch += [pltpu.SemaphoreType.DMA((size,)) for _, _, size, _ in parts]
    scratch.append(pltpu.SemaphoreType.DMA((len(parts),)))
    return pl.pallas_call(
        functools.partial(_exchange_kernel, layout),
        out_shape=tuple(shapes),
        in_specs=[pl.BlockSpec(memory_space=pl.ANY)] * len(parts),
        out_specs=tuple(pl.BlockSpec(memory_space=pl.ANY) for _ in parts),
        scratch_shapes=scratch,
        compiler_params=pltpu.CompilerParams(collective_id=collective_id, has_side_effects=True),
    )(*[array for array, _, _, _ in parts])


def _axis_sizes(n):
    y_size = 2
    x_size = 4
    z_size = n // (x_size * y_size)
    return z_size, x_size, y_size


def _column_cuts(width):
    lanes = width // 128
    first = (lanes + 2) // 3
    second = (lanes - first + 1) // 2
    return [0, first * 128, (first + second) * 128, width]


def reduce_rows(c, occ_axis, vir_axis):
    n = lax.axis_size(vir_axis)
    z_size, x_size, y_size = _axis_sizes(n)
    rows = c.shape[0] // n
    cuts = _column_cuts(c.shape[1])
    grid = c.reshape(z_size, x_size, y_size, rows, c.shape[1])
    axes = {"z": (x_size * y_size, z_size), "x": (y_size, x_size), "y": (1, y_size)}
    orders = [("z", "x", "y"), ("x", "y", "z"), ("y", "z", "x")]
    current = []
    for part, order in enumerate(orders):
        piece = grid[..., cuts[part]:cuts[part + 1]]
        perm = ["zxy".index(name) for name in order]
        current.append(jnp.transpose(piece, perm + [3, 4]))
    for stage in range(3):
        parts = []
        for part, order in enumerate(orders):
            stride, size = axes[order[stage]]
            parts.append((current[part], stride, size, False))
        arrived = exchange(parts, stage)
        current = [jnp.sum(block, axis=0) for block in arrived]
    return jnp.concatenate(current, axis=-1)


def gather_rows(block, occ_axis, vir_axis):
    n = lax.axis_size(vir_axis)
    z_size, x_size, y_size = _axis_sizes(n)
    cuts = _column_cuts(block.shape[-1])
    axes = {"z": (x_size * y_size, z_size), "x": (y_size, x_size), "y": (1, y_size)}
    orders = [("y", "x", "z"), ("z", "y", "x"), ("x", "z", "y")]
    current = [block[..., cuts[part]:cuts[part + 1]] for part in range(3)]
    for stage in range(3):
        parts = []
        for part, order in enumerate(orders):
            stride, size = axes[order[stage]]
            parts.append((current[part], stride, size, True))
        current = list(exchange(parts, 3 + stage))
    pieces = []
    for part, order in enumerate(orders):
        held = [order[2], order[1], order[0]]
        perm = [held.index(name) for name in "zxy"]
        arranged = jnp.transpose(current[part], [3] + perm + [4, 5])
        pairs, rows, cols = block.shape[0], block.shape[1], arranged.shape[-1]
        pieces.append(arranged.reshape(pairs, n * rows, cols))
    return jnp.concatenate(pieces, axis=-1)


def per_device(amplitudes, factors, occ_energy, vir_energy, occ_irrep, vir_irrep, pair_orbitals):
    local_pairs = amplitudes.shape[0]
    row_count = amplitudes.shape[1]
    occ_total = occ_energy.shape[0]
    occ_devices = lax.axis_size("occ")
    vir_devices = lax.axis_size("vir")
    occ_index = lax.axis_index("occ")
    vir_index = lax.axis_index("vir")
    lower_half = occ_index < occ_devices // 2

    outgoing = jnp.where(lower_half, amplitudes[1], amplitudes[0])
    incoming = passed_along(outgoing, "occ", occ_devices // 2)
    first = jnp.where(lower_half, amplitudes[0], incoming)
    second = jnp.where(lower_half, incoming, amplitudes[1])
    couple = jnp.stack([first, second], axis=0)
    gathered = gather_rows(couple, "occ", "vir")

    def half_product(factor):
        product = jnp.einsum("pcd,bd->pbc", gathered, factor, preferred_element_type=jnp.float32)
        return product.astype(jnp.bfloat16)

    halves = lax.map(half_product, factors)
    direct = jnp.einsum("qac,qbc->ab", factors, halves[:, 0], preferred_element_type=jnp.float32)
    turned_term = jnp.einsum("qac,qbc->ab", halves[:, 1], factors, preferred_element_type=jnp.float32)
    combined = direct + turned_term
    own_rows = reduce_rows(combined, "occ", "vir")
    cols = lax.all_to_all(own_rows, "vir", split_axis=1, concat_axis=0, tiled=True)
    own_cols = jnp.transpose(cols, (1, 0))
    outgoing_block = jnp.where(lower_half, own_cols, own_rows)
    incoming_block = passed_along(outgoing_block, "occ", occ_devices // 2)
    first_out = jnp.where(lower_half, own_rows, incoming_block)
    second_out = jnp.where(lower_half, incoming_block, own_cols)
    summed_pair = jnp.stack([first_out, second_out], axis=0)

    pair_ids = lax.dynamic_slice_in_dim(pair_orbitals, occ_index * local_pairs, local_pairs, 0)
    row_start = vir_index * row_count
    energy_rows = lax.dynamic_slice_in_dim(vir_energy, row_start, row_count, 0)
    irrep_rows = lax.dynamic_slice_in_dim(vir_irrep, row_start, row_count, 0)
    positions = jnp.arange(occ_total, dtype=jnp.int32)
    first_hot = positions[None, :] == pair_ids[:, 0:1]
    second_hot = positions[None, :] == pair_ids[:, 1:2]
    pair_energy = jnp.sum(jnp.where(first_hot, occ_energy[None, :], 0.0), axis=1) + jnp.sum(
        jnp.where(second_hot, occ_energy[None, :], 0.0), axis=1
    )
    first_irrep = jnp.sum(jnp.where(first_hot, occ_irrep[None, :], 0), axis=1)
    second_irrep = jnp.sum(jnp.where(second_hot, occ_irrep[None, :], 0), axis=1)
    pair_sym = jnp.bitwise_xor(first_irrep, second_irrep)
    combined_sym = jnp.bitwise_xor(
        jnp.bitwise_xor(pair_sym[:, None, None], irrep_rows[None, :, None]),
        vir_irrep[None, None, :],
    )
    allowed = combined_sym == 0
    denominator = (
        energy_rows[None, :, None] + vir_energy[None, None, :] - pair_energy[:, None, None]
    )
    return jnp.where(allowed, summed_pair / denominator, jnp.float32(0.0))


def solution(mesh):
    return jax.shard_map(
        per_device,
        mesh=mesh,
        in_specs=(P("occ", "vir", None), P("vir", None, None), P(), P(), P(), P(), P()),
        out_specs=P("occ", "vir", None),
        check_vma=False,
    )
```

```python
import jax
import jax.numpy as jnp
from jax import lax
from jax.sharding import PartitionSpec as P


def passed_along(block, axis, distance):
    devices = range(lax.axis_size(axis))
    route = [((i - distance) % len(devices), i) for i in devices]
    return lax.ppermute(block, axis, route)


def per_device(amplitudes, factors, occ_energy, vir_energy, occ_irrep, vir_irrep, pair_orbitals):
    local_pairs = amplitudes.shape[0]
    row_count = amplitudes.shape[1]
    occ_total = occ_energy.shape[0]
    occ_devices = lax.axis_size("occ")
    vir_devices = lax.axis_size("vir")
    occ_index = lax.axis_index("occ")
    vir_index = lax.axis_index("vir")
    lower_half = occ_index < occ_devices // 2

    outgoing = jnp.where(lower_half, amplitudes[1], amplitudes[0])
    incoming = passed_along(outgoing, "occ", occ_devices // 2)
    first = jnp.where(lower_half, amplitudes[0], incoming)
    second = jnp.where(lower_half, incoming, amplitudes[1])

    def gather_rows(block):
        spread = jnp.broadcast_to(block[None], (vir_devices,) + block.shape)
        pieces = lax.all_to_all(spread, "vir", split_axis=0, concat_axis=0, tiled=True)
        return pieces.reshape(vir_devices * row_count, block.shape[-1])

    def half_products(rows):
        def half_product(factor):
            product = jnp.einsum("cd,bd->bc", rows, factor, preferred_element_type=jnp.float32)
            return product.astype(jnp.bfloat16)

        return lax.map(half_product, factors)

    halves_first = half_products(gather_rows(first))
    halves_second = half_products(gather_rows(second))
    direct = jnp.einsum("qac,qbc->ab", factors, halves_first, preferred_element_type=jnp.float32)
    turned_term = jnp.einsum("qac,qbc->ab", halves_second, factors, preferred_element_type=jnp.float32)
    combined = direct + turned_term
    blocks = combined.reshape(vir_devices, row_count, combined.shape[-1])
    arrived = lax.all_to_all(blocks, "vir", split_axis=0, concat_axis=0, tiled=True)
    own_rows = jnp.sum(arrived, axis=0)
    cols = lax.all_to_all(own_rows, "vir", split_axis=1, concat_axis=0, tiled=True)
    own_cols = jnp.transpose(cols, (1, 0))
    outgoing_block = jnp.where(lower_half, own_cols, own_rows)
    incoming_block = passed_along(outgoing_block, "occ", occ_devices // 2)
    first_out = jnp.where(lower_half, own_rows, incoming_block)
    second_out = jnp.where(lower_half, incoming_block, own_cols)
    summed_pair = jnp.stack([first_out, second_out], axis=0)

    pair_ids = lax.dynamic_slice_in_dim(pair_orbitals, occ_index * local_pairs, local_pairs, 0)
    row_start = vir_index * row_count
    energy_rows = lax.dynamic_slice_in_dim(vir_energy, row_start, row_count, 0)
    irrep_rows = lax.dynamic_slice_in_dim(vir_irrep, row_start, row_count, 0)
    positions = jnp.arange(occ_total, dtype=jnp.int32)
    first_hot = positions[None, :] == pair_ids[:, 0:1]
    second_hot = positions[None, :] == pair_ids[:, 1:2]
    pair_energy = jnp.sum(jnp.where(first_hot, occ_energy[None, :], 0.0), axis=1) + jnp.sum(
        jnp.where(second_hot, occ_energy[None, :], 0.0), axis=1
    )
    first_irrep = jnp.sum(jnp.where(first_hot, occ_irrep[None, :], 0), axis=1)
    second_irrep = jnp.sum(jnp.where(second_hot, occ_irrep[None, :], 0), axis=1)
    pair_sym = jnp.bitwise_xor(first_irrep, second_irrep)
    combined_sym = jnp.bitwise_xor(
        jnp.bitwise_xor(pair_sym[:, None, None], irrep_rows[None, :, None]),
        vir_irrep[None, None, :],
    )
    allowed = combined_sym == 0
    denominator = (
        energy_rows[None, :, None] + vir_energy[None, None, :] - pair_energy[:, None, None]
    )
    return jnp.where(allowed, summed_pair / denominator, jnp.float32(0.0))


def solution(mesh):
    return jax.shard_map(
        per_device,
        mesh=mesh,
        in_specs=(P("occ", "vir", None), P("vir", None, None), P(), P(), P(), P(), P()),
        out_specs=P("occ", "vir", None),
        check_vma=False,
    )
```

```python
import functools

import jax
import jax.numpy as jnp
from jax import lax
from jax.sharding import PartitionSpec as P
from jax.experimental import pallas as pl
from jax.experimental.pallas import tpu as pltpu


def passed_along(block, axis, distance):
    devices = range(lax.axis_size(axis))
    route = [((i - distance) % len(devices), i) for i in devices]
    return lax.ppermute(block, axis, route)


def _ladder_scatter_kernel(n, groups, factors_ref, first_ref, second_ref, out_ref, cbuf, send_sems, recv_sems, own_sem):
    me = lax.axis_index("vir")
    group = lax.axis_index("occ")
    q_count = factors_ref.shape[0]
    rows = out_ref.shape[1]
    width = out_ref.shape[2]
    per_group = n // groups
    span = per_group * rows
    tile = min(256, width)
    tiles = width // tile
    dims = (((1,), (1,)), ((), ()))

    barrier = pltpu.get_barrier_semaphore()

    def greet(k, carry):
        pl.semaphore_signal(
            barrier, inc=1, device_id=(group, lax.rem(me + k, n)), device_id_type=pl.DeviceIdType.MESH
        )
        return carry

    lax.fori_loop(1, n, greet, 0)
    pl.semaphore_wait(barrier, n - 1)

    def remote(slot, i, dest):
        return pltpu.make_async_remote_copy(
            src_ref=cbuf.at[slot, pl.ds(i * rows, rows)],
            dst_ref=out_ref.at[me],
            send_sem=send_sems.at[dest],
            recv_sem=recv_sems.at[me],
            device_id=(group, dest),
            device_id_type=pl.DeviceIdType.MESH,
        )

    def local(slot, i):
        return pltpu.make_async_copy(cbuf.at[slot, pl.ds(i * rows, rows)], out_ref.at[me], own_sem)

    def group_at(step):
        return lax.rem(me // per_group + 1 + step, groups)

    def settle(step):
        slot = step % 2
        chosen = group_at(step)
        for i in range(per_group):
            dest = chosen * per_group + i

            @pl.when(dest != me)
            def _():
                remote(slot, i, dest).wait_send()

            @pl.when(dest == me)
            def _():
                local(slot, i).wait()

    for step in range(groups):
        slot = step % 2
        if step >= 2:
            settle(step - 2)
        chosen = group_at(step)
        row0 = pl.multiple_of(chosen * span, span)

        def product(t, carry):
            col0 = pl.multiple_of(t * tile, tile)
            acc = jnp.zeros((span, tile), jnp.float32)
            for q in range(q_count):
                acc += lax.dot_general(
                    factors_ref[q, pl.ds(row0, span), :], first_ref[q, pl.ds(col0, tile), :],
                    dims, preferred_element_type=jnp.float32,
                )
                acc += lax.dot_general(
                    second_ref[q, pl.ds(row0, span), :], factors_ref[q, pl.ds(col0, tile), :],
                    dims, preferred_element_type=jnp.float32,
                )
            cbuf[slot, :, pl.ds(col0, tile)] = acc
            return carry

        lax.fori_loop(0, tiles, product, 0)
        for i in range(per_group):
            dest = chosen * per_group + i

            @pl.when(dest != me)
            def _():
                remote(slot, i, dest).start()

            @pl.when(dest == me)
            def _():
                local(slot, i).start()

    for step in range(max(groups - 2, 0), groups):
        settle(step)

    def arrive(k, carry):
        source = lax.rem(me + k, n)
        pltpu.make_async_remote_copy(
            src_ref=cbuf.at[0, pl.ds(0, rows)],
            dst_ref=out_ref.at[source],
            send_sem=send_sems.at[source],
            recv_sem=recv_sems.at[source],
            device_id=(group, source),
            device_id_type=pl.DeviceIdType.MESH,
        ).wait_recv()
        return carry

    lax.fori_loop(1, n, arrive, 0)


def ladder_rows(factors, first_halves, second_halves, vir_axis):
    n = lax.axis_size(vir_axis)
    width = factors.shape[1]
    rows = width // n
    groups = 4
    arrived = pl.pallas_call(
        functools.partial(_ladder_scatter_kernel, n, groups),
        out_shape=jax.ShapeDtypeStruct((n, rows, width), jnp.float32),
        in_specs=[pl.BlockSpec(memory_space=pltpu.VMEM)] * 3,
        out_specs=pl.BlockSpec(memory_space=pl.ANY),
        scratch_shapes=[
            pltpu.VMEM((2, (n // groups) * rows, width), jnp.float32),
            pltpu.SemaphoreType.DMA((n,)),
            pltpu.SemaphoreType.DMA((n,)),
            pltpu.SemaphoreType.DMA,
        ],
        compiler_params=pltpu.CompilerParams(
            collective_id=0, has_side_effects=True, vmem_limit_bytes=48 * 1024 * 1024
        ),
    )(factors, first_halves, second_halves)
    return jnp.sum(arrived, axis=0)


def per_device(amplitudes, factors, occ_energy, vir_energy, occ_irrep, vir_irrep, pair_orbitals):
    local_pairs = amplitudes.shape[0]
    row_count = amplitudes.shape[1]
    occ_total = occ_energy.shape[0]
    occ_devices = lax.axis_size("occ")
    vir_devices = lax.axis_size("vir")
    occ_index = lax.axis_index("occ")
    vir_index = lax.axis_index("vir")
    lower_half = occ_index < occ_devices // 2

    outgoing = jnp.where(lower_half, amplitudes[1], amplitudes[0])
    incoming = passed_along(outgoing, "occ", occ_devices // 2)
    first = jnp.where(lower_half, amplitudes[0], incoming)
    second = jnp.where(lower_half, incoming, amplitudes[1])

    def gather_rows(block):
        spread = jnp.broadcast_to(block[None], (vir_devices,) + block.shape)
        pieces = lax.all_to_all(spread, "vir", split_axis=0, concat_axis=0, tiled=True)
        return pieces.reshape(vir_devices * row_count, block.shape[-1])

    def half_products(rows):
        def half_product(factor):
            product = jnp.einsum("cd,bd->bc", rows, factor, preferred_element_type=jnp.float32)
            return product.astype(jnp.bfloat16)

        return lax.map(half_product, factors)

    halves_first = half_products(gather_rows(first))
    halves_second = half_products(gather_rows(second))
    own_rows = ladder_rows(factors, halves_first, halves_second, "vir")
    cols = lax.all_to_all(own_rows, "vir", split_axis=1, concat_axis=0, tiled=True)
    own_cols = jnp.transpose(cols, (1, 0))
    outgoing_block = jnp.where(lower_half, own_cols, own_rows)
    incoming_block = passed_along(outgoing_block, "occ", occ_devices // 2)
    first_out = jnp.where(lower_half, own_rows, incoming_block)
    second_out = jnp.where(lower_half, incoming_block, own_cols)
    summed_pair = jnp.stack([first_out, second_out], axis=0)

    pair_ids = lax.dynamic_slice_in_dim(pair_orbitals, occ_index * local_pairs, local_pairs, 0)
    row_start = vir_index * row_count
    energy_rows = lax.dynamic_slice_in_dim(vir_energy, row_start, row_count, 0)
    irrep_rows = lax.dynamic_slice_in_dim(vir_irrep, row_start, row_count, 0)
    positions = jnp.arange(occ_total, dtype=jnp.int32)
    first_hot = positions[None, :] == pair_ids[:, 0:1]
    second_hot = positions[None, :] == pair_ids[:, 1:2]
    pair_energy = jnp.sum(jnp.where(first_hot, occ_energy[None, :], 0.0), axis=1) + jnp.sum(
        jnp.where(second_hot, occ_energy[None, :], 0.0), axis=1
    )
    first_irrep = jnp.sum(jnp.where(first_hot, occ_irrep[None, :], 0), axis=1)
    second_irrep = jnp.sum(jnp.where(second_hot, occ_irrep[None, :], 0), axis=1)
    pair_sym = jnp.bitwise_xor(first_irrep, second_irrep)
    combined_sym = jnp.bitwise_xor(
        jnp.bitwise_xor(pair_sym[:, None, None], irrep_rows[None, :, None]),
        vir_irrep[None, None, :],
    )
    allowed = combined_sym == 0
    denominator = (
        energy_rows[None, :, None] + vir_energy[None, None, :] - pair_energy[:, None, None]
    )
    return jnp.where(allowed, summed_pair / denominator, jnp.float32(0.0))


def solution(mesh):
    return jax.shard_map(
        per_device,
        mesh=mesh,
        in_specs=(P("occ", "vir", None), P("vir", None, None), P(), P(), P(), P(), P()),
        out_specs=P("occ", "vir", None),
        check_vma=False,
    )
```

```python
import jax
import jax.numpy as jnp
from jax import lax
from jax.sharding import PartitionSpec as P


def passed_along(block, axis, distance):
    devices = range(lax.axis_size(axis))
    route = [((i - distance) % len(devices), i) for i in devices]
    return lax.ppermute(block, axis, route)


def per_device(amplitudes, factors, occ_energy, vir_energy, occ_irrep, vir_irrep, pair_orbitals):
    local_pairs = amplitudes.shape[0]
    row_count = amplitudes.shape[1]
    occ_total = occ_energy.shape[0]
    occ_devices = lax.axis_size("occ")
    vir_devices = lax.axis_size("vir")
    occ_index = lax.axis_index("occ")
    vir_index = lax.axis_index("vir")
    lower_half = occ_index < occ_devices // 2

    own = jnp.where(lower_half, amplitudes[0], amplitudes[1])
    outgoing = jnp.where(lower_half, amplitudes[1], amplitudes[0])
    other = passed_along(outgoing, "occ", occ_devices // 2)

    def gather_rows(block):
        spread = jnp.broadcast_to(block[None], (vir_devices,) + block.shape)
        pieces = lax.all_to_all(spread, "vir", split_axis=0, concat_axis=0, tiled=True)
        return pieces.reshape(vir_devices * row_count, block.shape[-1])

    def half_products(rows):
        product = jnp.einsum("cd,qbd->qbc", rows, factors, preferred_element_type=jnp.float32)
        return product.astype(jnp.bfloat16)

    halves_first = half_products(gather_rows(own))
    halves_second = half_products(gather_rows(other))
    direct = jnp.einsum("qac,qbc->ab", factors, halves_first, preferred_element_type=jnp.float32)
    turned_term = jnp.einsum("qac,qbc->ab", halves_second, factors, preferred_element_type=jnp.float32)
    combined = direct + turned_term
    blocks = combined.reshape(vir_devices, row_count, combined.shape[-1])
    arrived = lax.all_to_all(blocks, "vir", split_axis=0, concat_axis=0, tiled=True)
    own_rows = jnp.sum(arrived, axis=0)
    cols = lax.all_to_all(own_rows, "vir", split_axis=1, concat_axis=0, tiled=True)
    own_cols = jnp.transpose(cols, (1, 0))
    partner_cols = passed_along(own_cols, "occ", occ_devices // 2)
    first_out = jnp.where(lower_half, own_rows, partner_cols)
    second_out = jnp.where(lower_half, partner_cols, own_rows)
    summed_pair = jnp.stack([first_out, second_out], axis=0)

    pair_ids = lax.dynamic_slice_in_dim(pair_orbitals, occ_index * local_pairs, local_pairs, 0)
    row_start = vir_index * row_count
    energy_rows = lax.dynamic_slice_in_dim(vir_energy, row_start, row_count, 0)
    irrep_rows = lax.dynamic_slice_in_dim(vir_irrep, row_start, row_count, 0)
    positions = jnp.arange(occ_total, dtype=jnp.int32)
    first_hot = positions[None, :] == pair_ids[:, 0:1]
    second_hot = positions[None, :] == pair_ids[:, 1:2]
    pair_energy = jnp.sum(jnp.where(first_hot, occ_energy[None, :], 0.0), axis=1) + jnp.sum(
        jnp.where(second_hot, occ_energy[None, :], 0.0), axis=1
    )
    first_irrep = jnp.sum(jnp.where(first_hot, occ_irrep[None, :], 0), axis=1)
    second_irrep = jnp.sum(jnp.where(second_hot, occ_irrep[None, :], 0), axis=1)
    pair_sym = jnp.bitwise_xor(first_irrep, second_irrep)
    combined_sym = jnp.bitwise_xor(
        jnp.bitwise_xor(pair_sym[:, None, None], irrep_rows[None, :, None]),
        vir_irrep[None, None, :],
    )
    allowed = combined_sym == 0
    denominator = (
        energy_rows[None, :, None] + vir_energy[None, None, :] - pair_energy[:, None, None]
    )
    return jnp.where(allowed, summed_pair / denominator, jnp.float32(0.0))


def solution(mesh):
    return jax.shard_map(
        per_device,
        mesh=mesh,
        in_specs=(P("occ", "vir", None), P("vir", None, None), P(), P(), P(), P(), P()),
        out_specs=P("occ", "vir", None),
        check_vma=False,
    )
```

```python
import functools

import jax
import jax.numpy as jnp
from jax import lax
from jax.sharding import PartitionSpec as P
from jax.experimental import pallas as pl
from jax.experimental.pallas import tpu as pltpu


def passed_along(block, axis, distance):
    devices = range(lax.axis_size(axis))
    route = [((i - distance) % len(devices), i) for i in devices]
    return lax.ppermute(block, axis, route)


def _turn_kernel(n, blocks_ref, out_ref, send_sems, recv_sems):
    me = lax.axis_index("vir")
    group = lax.axis_index("occ")
    partner = lax.rem(group + lax.axis_size("occ") // 2, lax.axis_size("occ"))

    barrier = pltpu.get_barrier_semaphore()

    def greet(k, carry):
        pl.semaphore_signal(barrier, inc=1, device_id=(partner, k), device_id_type=pl.DeviceIdType.MESH)
        return carry

    lax.fori_loop(0, n, greet, 0)
    pl.semaphore_wait(barrier, n)

    def copy_to(k):
        dest = lax.rem(me + k, n)
        return pltpu.make_async_remote_copy(
            src_ref=blocks_ref.at[dest],
            dst_ref=out_ref.at[me],
            send_sem=send_sems.at[dest],
            recv_sem=recv_sems.at[me],
            device_id=(partner, dest),
            device_id_type=pl.DeviceIdType.MESH,
        )

    def send(k, carry):
        copy_to(k).start()
        return carry

    lax.fori_loop(0, n, send, 0)

    def finish(k, carry):
        copy_to(k).wait_send()
        source = lax.rem(me + n - k, n)
        pltpu.make_async_remote_copy(
            src_ref=blocks_ref.at[source],
            dst_ref=out_ref.at[source],
            send_sem=send_sems.at[source],
            recv_sem=recv_sems.at[source],
            device_id=(partner, source),
            device_id_type=pl.DeviceIdType.MESH,
        ).wait_recv()
        return carry

    lax.fori_loop(0, n, finish, 0)


def partner_transpose(own_rows, vir_axis):
    n = lax.axis_size(vir_axis)
    rows, width = own_rows.shape
    blocks = jnp.transpose(own_rows.reshape(rows, n, width // n), (1, 2, 0))
    arrived = pl.pallas_call(
        functools.partial(_turn_kernel, n),
        out_shape=jax.ShapeDtypeStruct(blocks.shape, blocks.dtype),
        in_specs=[pl.BlockSpec(memory_space=pl.ANY)],
        out_specs=pl.BlockSpec(memory_space=pl.ANY),
        scratch_shapes=[pltpu.SemaphoreType.DMA((n,)), pltpu.SemaphoreType.DMA((n,))],
        compiler_params=pltpu.CompilerParams(collective_id=1, has_side_effects=True),
    )(blocks)
    return jnp.transpose(arrived, (1, 0, 2)).reshape(width // n, n * rows)


def per_device(amplitudes, factors, occ_energy, vir_energy, occ_irrep, vir_irrep, pair_orbitals):
    local_pairs = amplitudes.shape[0]
    row_count = amplitudes.shape[1]
    occ_total = occ_energy.shape[0]
    occ_devices = lax.axis_size("occ")
    vir_devices = lax.axis_size("vir")
    occ_index = lax.axis_index("occ")
    vir_index = lax.axis_index("vir")
    lower_half = occ_index < occ_devices // 2

    own = jnp.where(lower_half, amplitudes[0], amplitudes[1])
    outgoing = jnp.where(lower_half, amplitudes[1], amplitudes[0])
    other = passed_along(outgoing, "occ", occ_devices // 2)
    own, other = lax.optimization_barrier((own, other))

    def gather_rows(block):
        spread = jnp.broadcast_to(block[None], (vir_devices,) + block.shape)
        pieces = lax.all_to_all(spread, "vir", split_axis=0, concat_axis=0, tiled=True)
        return pieces.reshape(vir_devices * row_count, block.shape[-1])

    def half_products(rows):
        product = jnp.einsum("cd,qbd->qbc", rows, factors, preferred_element_type=jnp.float32)
        return product.astype(jnp.bfloat16)

    halves_first = half_products(gather_rows(own))
    halves_second = half_products(gather_rows(other))
    direct = jnp.einsum("qac,qbc->ab", factors, halves_first, preferred_element_type=jnp.float32)
    turned_term = jnp.einsum("qac,qbc->ab", halves_second, factors, preferred_element_type=jnp.float32)
    combined = direct + turned_term
    blocks = combined.reshape(vir_devices, row_count, combined.shape[-1])
    arrived = lax.all_to_all(blocks, "vir", split_axis=0, concat_axis=0, tiled=True)
    own_rows = jnp.sum(arrived, axis=0)
    partner_cols = partner_transpose(own_rows, "vir")
    first_out = jnp.where(lower_half, own_rows, partner_cols)
    second_out = jnp.where(lower_half, partner_cols, own_rows)
    summed_pair = jnp.stack([first_out, second_out], axis=0)

    pair_ids = lax.dynamic_slice_in_dim(pair_orbitals, occ_index * local_pairs, local_pairs, 0)
    row_start = vir_index * row_count
    energy_rows = lax.dynamic_slice_in_dim(vir_energy, row_start, row_count, 0)
    irrep_rows = lax.dynamic_slice_in_dim(vir_irrep, row_start, row_count, 0)
    positions = jnp.arange(occ_total, dtype=jnp.int32)
    first_hot = positions[None, :] == pair_ids[:, 0:1]
    second_hot = positions[None, :] == pair_ids[:, 1:2]
    pair_energy = jnp.sum(jnp.where(first_hot, occ_energy[None, :], 0.0), axis=1) + jnp.sum(
        jnp.where(second_hot, occ_energy[None, :], 0.0), axis=1
    )
    first_irrep = jnp.sum(jnp.where(first_hot, occ_irrep[None, :], 0), axis=1)
    second_irrep = jnp.sum(jnp.where(second_hot, occ_irrep[None, :], 0), axis=1)
    pair_sym = jnp.bitwise_xor(first_irrep, second_irrep)
    combined_sym = jnp.bitwise_xor(
        jnp.bitwise_xor(pair_sym[:, None, None], irrep_rows[None, :, None]),
        vir_irrep[None, None, :],
    )
    allowed = combined_sym == 0
    denominator = (
        energy_rows[None, :, None] + vir_energy[None, None, :] - pair_energy[:, None, None]
    )
    return jnp.where(allowed, summed_pair / denominator, jnp.float32(0.0))


def solution(mesh):
    return jax.shard_map(
        per_device,
        mesh=mesh,
        in_specs=(P("occ", "vir", None), P("vir", None, None), P(), P(), P(), P(), P()),
        out_specs=P("occ", "vir", None),
        check_vma=False,
    )
```

```python
import functools

import jax
import jax.numpy as jnp
from jax import lax
from jax.sharding import PartitionSpec as P
from jax.experimental import pallas as pl
from jax.experimental.pallas import tpu as pltpu


def passed_along(block, axis, distance):
    devices = range(lax.axis_size(axis))
    route = [((i - distance) % len(devices), i) for i in devices]
    return lax.ppermute(block, axis, route)


def _turn_kernel(n, blocks_ref, out_ref, send_sems, recv_sems):
    me = lax.axis_index("vir")
    group = lax.axis_index("occ")
    partner = lax.rem(group + lax.axis_size("occ") // 2, lax.axis_size("occ"))

    barrier = pltpu.get_barrier_semaphore()

    def greet(k, carry):
        pl.semaphore_signal(barrier, inc=1, device_id=(partner, k), device_id_type=pl.DeviceIdType.MESH)
        return carry

    lax.fori_loop(0, n, greet, 0)
    pl.semaphore_wait(barrier, n)

    def copy_to(k):
        dest = lax.rem(me + k, n)
        return pltpu.make_async_remote_copy(
            src_ref=blocks_ref.at[dest],
            dst_ref=out_ref.at[me],
            send_sem=send_sems.at[dest],
            recv_sem=recv_sems.at[me],
            device_id=(partner, dest),
            device_id_type=pl.DeviceIdType.MESH,
        )

    def send(k, carry):
        copy_to(k).start()
        return carry

    lax.fori_loop(0, n, send, 0)

    def finish(k, carry):
        copy_to(k).wait_send()
        source = lax.rem(me + n - k, n)
        pltpu.make_async_remote_copy(
            src_ref=blocks_ref.at[source],
            dst_ref=out_ref.at[source],
            send_sem=send_sems.at[source],
            recv_sem=recv_sems.at[source],
            device_id=(partner, source),
            device_id_type=pl.DeviceIdType.MESH,
        ).wait_recv()
        return carry

    lax.fori_loop(0, n, finish, 0)


def partner_transpose(own_rows, vir_axis):
    n = lax.axis_size(vir_axis)
    rows, width = own_rows.shape
    blocks = jnp.transpose(own_rows.reshape(rows, n, width // n), (1, 2, 0))
    arrived = pl.pallas_call(
        functools.partial(_turn_kernel, n),
        out_shape=jax.ShapeDtypeStruct(blocks.shape, blocks.dtype),
        in_specs=[pl.BlockSpec(memory_space=pl.ANY)],
        out_specs=pl.BlockSpec(memory_space=pl.ANY),
        scratch_shapes=[pltpu.SemaphoreType.DMA((n,)), pltpu.SemaphoreType.DMA((n,))],
        compiler_params=pltpu.CompilerParams(collective_id=1, has_side_effects=True),
    )(blocks)
    return jnp.transpose(arrived, (1, 0, 2)).reshape(width // n, n * rows)


def per_device(amplitudes, factors, occ_energy, vir_energy, occ_irrep, vir_irrep, pair_orbitals):
    local_pairs = amplitudes.shape[0]
    row_count = amplitudes.shape[1]
    occ_total = occ_energy.shape[0]
    occ_devices = lax.axis_size("occ")
    vir_devices = lax.axis_size("vir")
    occ_index = lax.axis_index("occ")
    vir_index = lax.axis_index("vir")
    lower_half = occ_index < occ_devices // 2

    own = jnp.where(lower_half, amplitudes[0], amplitudes[1])
    outgoing = jnp.where(lower_half, amplitudes[1], amplitudes[0])
    other = passed_along(outgoing, "occ", occ_devices // 2)
    own, other = lax.optimization_barrier((own, other))

    def gather_rows(block):
        spread = jnp.broadcast_to(block[None], (vir_devices,) + block.shape)
        pieces = lax.all_to_all(spread, "vir", split_axis=0, concat_axis=0, tiled=True)
        return pieces.reshape(vir_devices * row_count, block.shape[-1])

    def half_products(rows):
        product = jnp.einsum("cd,qbd->qbc", rows, factors, preferred_element_type=jnp.float32)
        return product.astype(jnp.bfloat16)

    halves_first = half_products(gather_rows(own))
    halves_second = half_products(gather_rows(other))
    direct = jnp.einsum("qac,qbc->ab", factors, halves_first, preferred_element_type=jnp.float32)
    turned_term = jnp.einsum("qac,qbc->ab", halves_second, factors, preferred_element_type=jnp.float32)
    combined = direct + turned_term
    blocks = combined.reshape(vir_devices, row_count, combined.shape[-1]).astype(jnp.bfloat16)
    arrived = lax.all_to_all(blocks, "vir", split_axis=0, concat_axis=0, tiled=True)
    own_rows = jnp.sum(arrived.astype(jnp.float32), axis=0)
    partner_cols = partner_transpose(own_rows, "vir")
    first_out = jnp.where(lower_half, own_rows, partner_cols)
    second_out = jnp.where(lower_half, partner_cols, own_rows)
    summed_pair = jnp.stack([first_out, second_out], axis=0)

    pair_ids = lax.dynamic_slice_in_dim(pair_orbitals, occ_index * local_pairs, local_pairs, 0)
    row_start = vir_index * row_count
    energy_rows = lax.dynamic_slice_in_dim(vir_energy, row_start, row_count, 0)
    irrep_rows = lax.dynamic_slice_in_dim(vir_irrep, row_start, row_count, 0)
    positions = jnp.arange(occ_total, dtype=jnp.int32)
    first_hot = positions[None, :] == pair_ids[:, 0:1]
    second_hot = positions[None, :] == pair_ids[:, 1:2]
    pair_energy = jnp.sum(jnp.where(first_hot, occ_energy[None, :], 0.0), axis=1) + jnp.sum(
        jnp.where(second_hot, occ_energy[None, :], 0.0), axis=1
    )
    first_irrep = jnp.sum(jnp.where(first_hot, occ_irrep[None, :], 0), axis=1)
    second_irrep = jnp.sum(jnp.where(second_hot, occ_irrep[None, :], 0), axis=1)
    pair_sym = jnp.bitwise_xor(first_irrep, second_irrep)
    combined_sym = jnp.bitwise_xor(
        jnp.bitwise_xor(pair_sym[:, None, None], irrep_rows[None, :, None]),
        vir_irrep[None, None, :],
    )
    allowed = combined_sym == 0
    denominator = (
        energy_rows[None, :, None] + vir_energy[None, None, :] - pair_energy[:, None, None]
    )
    return jnp.where(allowed, summed_pair / denominator, jnp.float32(0.0))


def solution(mesh):
    return jax.shard_map(
        per_device,
        mesh=mesh,
        in_specs=(P("occ", "vir", None), P("vir", None, None), P(), P(), P(), P(), P()),
        out_specs=P("occ", "vir", None),
        check_vma=False,
    )
```

```python
import functools

import jax
import jax.numpy as jnp
from jax import lax
from jax.sharding import PartitionSpec as P
from jax.experimental import pallas as pl
from jax.experimental.pallas import tpu as pltpu


def passed_along(block, axis, distance):
    devices = range(lax.axis_size(axis))
    route = [((i - distance) % len(devices), i) for i in devices]
    return lax.ppermute(block, axis, route)


def _turn_kernel(n, blocks_ref, out_ref, send_sems, recv_sems):
    me = lax.axis_index("vir")
    group = lax.axis_index("occ")
    partner = lax.rem(group + lax.axis_size("occ") // 2, lax.axis_size("occ"))

    barrier = pltpu.get_barrier_semaphore()

    def greet(k, carry):
        pl.semaphore_signal(barrier, inc=1, device_id=(partner, k), device_id_type=pl.DeviceIdType.MESH)
        return carry

    lax.fori_loop(0, n, greet, 0)
    pl.semaphore_wait(barrier, n)

    def copy_to(k):
        dest = lax.rem(me + k, n)
        return pltpu.make_async_remote_copy(
            src_ref=blocks_ref.at[dest],
            dst_ref=out_ref.at[me],
            send_sem=send_sems.at[dest],
            recv_sem=recv_sems.at[me],
            device_id=(partner, dest),
            device_id_type=pl.DeviceIdType.MESH,
        )

    def send(k, carry):
        copy_to(k).start()
        return carry

    lax.fori_loop(0, n, send, 0)

    def finish(k, carry):
        copy_to(k).wait_send()
        source = lax.rem(me + n - k, n)
        pltpu.make_async_remote_copy(
            src_ref=blocks_ref.at[source],
            dst_ref=out_ref.at[source],
            send_sem=send_sems.at[source],
            recv_sem=recv_sems.at[source],
            device_id=(partner, source),
            device_id_type=pl.DeviceIdType.MESH,
        ).wait_recv()
        return carry

    lax.fori_loop(0, n, finish, 0)


def partner_transpose(own_rows, vir_axis):
    n = lax.axis_size(vir_axis)
    rows, width = own_rows.shape
    blocks = jnp.transpose(own_rows.reshape(rows, n, width // n), (1, 2, 0))
    arrived = pl.pallas_call(
        functools.partial(_turn_kernel, n),
        out_shape=jax.ShapeDtypeStruct(blocks.shape, blocks.dtype),
        in_specs=[pl.BlockSpec(memory_space=pl.ANY)],
        out_specs=pl.BlockSpec(memory_space=pl.ANY),
        scratch_shapes=[pltpu.SemaphoreType.DMA((n,)), pltpu.SemaphoreType.DMA((n,))],
        compiler_params=pltpu.CompilerParams(collective_id=1, has_side_effects=True),
    )(blocks)
    return jnp.transpose(arrived, (1, 0, 2)).reshape(width // n, n * rows)


def per_device(amplitudes, factors, occ_energy, vir_energy, occ_irrep, vir_irrep, pair_orbitals):
    local_pairs = amplitudes.shape[0]
    row_count = amplitudes.shape[1]
    occ_total = occ_energy.shape[0]
    occ_devices = lax.axis_size("occ")
    vir_devices = lax.axis_size("vir")
    occ_index = lax.axis_index("occ")
    vir_index = lax.axis_index("vir")
    lower_half = occ_index < occ_devices // 2

    own = jnp.where(lower_half, amplitudes[0], amplitudes[1])
    outgoing = jnp.where(lower_half, amplitudes[1], amplitudes[0])
    other = passed_along(outgoing, "occ", occ_devices // 2)

    def gather_rows(block):
        spread = jnp.broadcast_to(block[None], (vir_devices,) + block.shape)
        pieces = lax.all_to_all(spread, "vir", split_axis=0, concat_axis=0, tiled=True)
        return pieces.reshape(vir_devices * row_count, block.shape[-1])

    def half_products(rows):
        product = jnp.einsum("cd,qbd->qbc", rows, factors, preferred_element_type=jnp.float32)
        return product.astype(jnp.bfloat16)

    halves_first = half_products(lax.all_gather(own, "vir", axis=0, tiled=True))
    halves_second = half_products(gather_rows(other))
    direct = jnp.einsum("qac,qbc->ab", factors, halves_first, preferred_element_type=jnp.float32)
    turned_term = jnp.einsum("qac,qbc->ab", halves_second, factors, preferred_element_type=jnp.float32)
    combined = direct + turned_term
    blocks = combined.reshape(vir_devices, row_count, combined.shape[-1]).astype(jnp.bfloat16)
    arrived = lax.all_to_all(blocks, "vir", split_axis=0, concat_axis=0, tiled=True)
    own_rows = jnp.sum(arrived.astype(jnp.float32), axis=0)
    partner_cols = partner_transpose(own_rows, "vir")
    first_out = jnp.where(lower_half, own_rows, partner_cols)
    second_out = jnp.where(lower_half, partner_cols, own_rows)
    summed_pair = jnp.stack([first_out, second_out], axis=0)

    pair_ids = lax.dynamic_slice_in_dim(pair_orbitals, occ_index * local_pairs, local_pairs, 0)
    row_start = vir_index * row_count
    energy_rows = lax.dynamic_slice_in_dim(vir_energy, row_start, row_count, 0)
    irrep_rows = lax.dynamic_slice_in_dim(vir_irrep, row_start, row_count, 0)
    positions = jnp.arange(occ_total, dtype=jnp.int32)
    first_hot = positions[None, :] == pair_ids[:, 0:1]
    second_hot = positions[None, :] == pair_ids[:, 1:2]
    pair_energy = jnp.sum(jnp.where(first_hot, occ_energy[None, :], 0.0), axis=1) + jnp.sum(
        jnp.where(second_hot, occ_energy[None, :], 0.0), axis=1
    )
    first_irrep = jnp.sum(jnp.where(first_hot, occ_irrep[None, :], 0), axis=1)
    second_irrep = jnp.sum(jnp.where(second_hot, occ_irrep[None, :], 0), axis=1)
    pair_sym = jnp.bitwise_xor(first_irrep, second_irrep)
    combined_sym = jnp.bitwise_xor(
        jnp.bitwise_xor(pair_sym[:, None, None], irrep_rows[None, :, None]),
        vir_irrep[None, None, :],
    )
    allowed = combined_sym == 0
    denominator = (
        energy_rows[None, :, None] + vir_energy[None, None, :] - pair_energy[:, None, None]
    )
    return jnp.where(allowed, summed_pair / denominator, jnp.float32(0.0))


def solution(mesh):
    return jax.shard_map(
        per_device,
        mesh=mesh,
        in_specs=(P("occ", "vir", None), P("vir", None, None), P(), P(), P(), P(), P()),
        out_specs=P("occ", "vir", None),
        check_vma=False,
    )
```

```python
import functools

import jax
import jax.numpy as jnp
from jax import lax
from jax.sharding import PartitionSpec as P
from jax.experimental import pallas as pl
from jax.experimental.pallas import tpu as pltpu


def passed_along(block, axis, distance):
    devices = range(lax.axis_size(axis))
    route = [((i - distance) % len(devices), i) for i in devices]
    return lax.ppermute(block, axis, route)


def _scatter_turn_kernel(n, parts_ref, own_ref, turned_ref, slots, flipped, sems):
    me = lax.axis_index("vir")
    group = lax.axis_index("occ")
    partner = lax.rem(group + lax.axis_size("occ") // 2, lax.axis_size("occ"))
    rs_send, rs_recv, local_sem, t_send, t_recv = sems
    rows = own_ref.shape[0]

    barrier = pltpu.get_barrier_semaphore()

    def greet(k, carry):
        pl.semaphore_signal(barrier, inc=1, device_id=(partner, k), device_id_type=pl.DeviceIdType.MESH)

        @pl.when(k != me)
        def _():
            pl.semaphore_signal(barrier, inc=1, device_id=(group, k), device_id_type=pl.DeviceIdType.MESH)

        return carry

    lax.fori_loop(0, n, greet, 0)
    pl.semaphore_wait(barrier, 2 * n - 1)

    def part_copy(dest):
        return pltpu.make_async_remote_copy(
            src_ref=parts_ref.at[dest],
            dst_ref=slots.at[me],
            send_sem=rs_send.at[dest],
            recv_sem=rs_recv.at[me],
            device_id=(group, dest),
            device_id_type=pl.DeviceIdType.MESH,
        )

    local = pltpu.make_async_copy(parts_ref.at[me], slots.at[me], local_sem)
    local.start()

    def send(k, carry):
        part_copy(lax.rem(me + k, n)).start()
        return carry

    lax.fori_loop(1, n, send, 0)

    def settle(k, carry):
        part_copy(lax.rem(me + k, n)).wait_send()
        source = lax.rem(me + n - k, n)
        pltpu.make_async_remote_copy(
            src_ref=parts_ref.at[source],
            dst_ref=slots.at[source],
            send_sem=rs_send.at[source],
            recv_sem=rs_recv.at[source],
            device_id=(group, source),
            device_id_type=pl.DeviceIdType.MESH,
        ).wait_recv()
        return carry

    lax.fori_loop(1, n, settle, 0)
    local.wait()

    def accumulate(w, total):
        return total + slots[w].astype(jnp.float32)

    total = lax.fori_loop(0, n, accumulate, jnp.zeros(own_ref.shape, jnp.float32))
    own_ref[...] = total
    flipped[...] = jnp.transpose(total, (1, 0))

    def turn_copy(dest):
        return pltpu.make_async_remote_copy(
            src_ref=flipped.at[pl.ds(pl.multiple_of(dest * rows, rows), rows)],
            dst_ref=turned_ref.at[me],
            send_sem=t_send.at[dest],
            recv_sem=t_recv.at[me],
            device_id=(partner, dest),
            device_id_type=pl.DeviceIdType.MESH,
        )

    def turn(k, carry):
        turn_copy(k).start()
        return carry

    lax.fori_loop(0, n, turn, 0)

    def finish(k, carry):
        turn_copy(k).wait_send()
        pltpu.make_async_remote_copy(
            src_ref=flipped.at[pl.ds(pl.multiple_of(k * rows, rows), rows)],
            dst_ref=turned_ref.at[k],
            send_sem=t_send.at[k],
            recv_sem=t_recv.at[k],
            device_id=(partner, k),
            device_id_type=pl.DeviceIdType.MESH,
        ).wait_recv()
        return carry

    lax.fori_loop(0, n, finish, 0)


def scatter_and_turn(parts, vir_axis):
    n = lax.axis_size(vir_axis)
    rows, width = parts.shape[1], parts.shape[2]
    own_rows, arrived = pl.pallas_call(
        functools.partial(_scatter_turn_kernel, n),
        out_shape=(
            jax.ShapeDtypeStruct((rows, width), jnp.float32),
            jax.ShapeDtypeStruct((n, rows, rows), jnp.float32),
        ),
        in_specs=[pl.BlockSpec(memory_space=pl.ANY)],
        out_specs=(pl.BlockSpec(memory_space=pltpu.VMEM), pl.BlockSpec(memory_space=pl.ANY)),
        scratch_shapes=[
            pltpu.VMEM((n, rows, width), parts.dtype),
            pltpu.VMEM((width, rows), jnp.float32),
            (
                pltpu.SemaphoreType.DMA((n,)),
                pltpu.SemaphoreType.DMA((n,)),
                pltpu.SemaphoreType.DMA,
                pltpu.SemaphoreType.DMA((n,)),
                pltpu.SemaphoreType.DMA((n,)),
            ),
        ],
        compiler_params=pltpu.CompilerParams(collective_id=1, has_side_effects=True),
    )(parts)
    partner_cols = jnp.transpose(arrived, (1, 0, 2)).reshape(rows, n * rows)
    return own_rows, partner_cols


def per_device(amplitudes, factors, occ_energy, vir_energy, occ_irrep, vir_irrep, pair_orbitals):
    local_pairs = amplitudes.shape[0]
    row_count = amplitudes.shape[1]
    occ_total = occ_energy.shape[0]
    occ_devices = lax.axis_size("occ")
    vir_devices = lax.axis_size("vir")
    occ_index = lax.axis_index("occ")
    vir_index = lax.axis_index("vir")
    lower_half = occ_index < occ_devices // 2

    own = jnp.where(lower_half, amplitudes[0], amplitudes[1])
    outgoing = jnp.where(lower_half, amplitudes[1], amplitudes[0])
    other = passed_along(outgoing, "occ", occ_devices // 2)
    own, other = lax.optimization_barrier((own, other))

    def gather_rows(block):
        spread = jnp.broadcast_to(block[None], (vir_devices,) + block.shape)
        pieces = lax.all_to_all(spread, "vir", split_axis=0, concat_axis=0, tiled=True)
        return pieces.reshape(vir_devices * row_count, block.shape[-1])

    def half_products(rows):
        product = jnp.einsum("cd,qbd->qbc", rows, factors, preferred_element_type=jnp.float32)
        return product.astype(jnp.bfloat16)

    halves_first = half_products(gather_rows(own))
    halves_second = half_products(gather_rows(other))
    direct = jnp.einsum("qac,qbc->ab", factors, halves_first, preferred_element_type=jnp.float32)
    turned_term = jnp.einsum("qac,qbc->ab", halves_second, factors, preferred_element_type=jnp.float32)
    combined = direct + turned_term
    blocks = combined.reshape(vir_devices, row_count, combined.shape[-1]).astype(jnp.bfloat16)
    own_rows, partner_cols = scatter_and_turn(blocks, "vir")
    first_out = jnp.where(lower_half, own_rows, partner_cols)
    second_out = jnp.where(lower_half, partner_cols, own_rows)
    summed_pair = jnp.stack([first_out, second_out], axis=0)

    pair_ids = lax.dynamic_slice_in_dim(pair_orbitals, occ_index * local_pairs, local_pairs, 0)
    row_start = vir_index * row_count
    energy_rows = lax.dynamic_slice_in_dim(vir_energy, row_start, row_count, 0)
    irrep_rows = lax.dynamic_slice_in_dim(vir_irrep, row_start, row_count, 0)
    positions = jnp.arange(occ_total, dtype=jnp.int32)
    first_hot = positions[None, :] == pair_ids[:, 0:1]
    second_hot = positions[None, :] == pair_ids[:, 1:2]
    pair_energy = jnp.sum(jnp.where(first_hot, occ_energy[None, :], 0.0), axis=1) + jnp.sum(
        jnp.where(second_hot, occ_energy[None, :], 0.0), axis=1
    )
    first_irrep = jnp.sum(jnp.where(first_hot, occ_irrep[None, :], 0), axis=1)
    second_irrep = jnp.sum(jnp.where(second_hot, occ_irrep[None, :], 0), axis=1)
    pair_sym = jnp.bitwise_xor(first_irrep, second_irrep)
    combined_sym = jnp.bitwise_xor(
        jnp.bitwise_xor(pair_sym[:, None, None], irrep_rows[None, :, None]),
        vir_irrep[None, None, :],
    )
    allowed = combined_sym == 0
    denominator = (
        energy_rows[None, :, None] + vir_energy[None, None, :] - pair_energy[:, None, None]
    )
    return jnp.where(allowed, summed_pair / denominator, jnp.float32(0.0))


def solution(mesh):
    return jax.shard_map(
        per_device,
        mesh=mesh,
        in_specs=(P("occ", "vir", None), P("vir", None, None), P(), P(), P(), P(), P()),
        out_specs=P("occ", "vir", None),
        check_vma=False,
    )
```

```python
import functools

import jax
import jax.numpy as jnp
from jax import lax
from jax.sharding import PartitionSpec as P
from jax.experimental import pallas as pl
from jax.experimental.pallas import tpu as pltpu


def passed_along(block, axis, distance):
    devices = range(lax.axis_size(axis))
    route = [((i - distance) % len(devices), i) for i in devices]
    return lax.ppermute(block, axis, route)


def _turn_kernel(n, blocks_ref, out_ref, send_sems, recv_sems):
    me = lax.axis_index("vir")
    group = lax.axis_index("occ")
    partner = lax.rem(group + lax.axis_size("occ") // 2, lax.axis_size("occ"))

    barrier = pltpu.get_barrier_semaphore()

    def greet(k, carry):
        pl.semaphore_signal(barrier, inc=1, device_id=(partner, k), device_id_type=pl.DeviceIdType.MESH)
        return carry

    lax.fori_loop(0, n, greet, 0)
    pl.semaphore_wait(barrier, n)

    def copy_to(k):
        dest = lax.rem(me + k, n)
        return pltpu.make_async_remote_copy(
            src_ref=blocks_ref.at[dest],
            dst_ref=out_ref.at[me],
            send_sem=send_sems.at[dest],
            recv_sem=recv_sems.at[me],
            device_id=(partner, dest),
            device_id_type=pl.DeviceIdType.MESH,
        )

    def send(k, carry):
        copy_to(k).start()
        return carry

    lax.fori_loop(0, n, send, 0)

    def finish(k, carry):
        copy_to(k).wait_send()
        source = lax.rem(me + n - k, n)
        pltpu.make_async_remote_copy(
            src_ref=blocks_ref.at[source],
            dst_ref=out_ref.at[source],
            send_sem=send_sems.at[source],
            recv_sem=recv_sems.at[source],
            device_id=(partner, source),
            device_id_type=pl.DeviceIdType.MESH,
        ).wait_recv()
        return carry

    lax.fori_loop(0, n, finish, 0)


def partner_transpose(own_rows, vir_axis):
    n = lax.axis_size(vir_axis)
    rows, width = own_rows.shape
    blocks = jnp.transpose(own_rows.reshape(rows, n, width // n), (1, 2, 0))
    arrived = pl.pallas_call(
        functools.partial(_turn_kernel, n),
        out_shape=jax.ShapeDtypeStruct(blocks.shape, blocks.dtype),
        in_specs=[pl.BlockSpec(memory_space=pl.ANY)],
        out_specs=pl.BlockSpec(memory_space=pl.ANY),
        scratch_shapes=[pltpu.SemaphoreType.DMA((n,)), pltpu.SemaphoreType.DMA((n,))],
        compiler_params=pltpu.CompilerParams(collective_id=1, has_side_effects=True),
    )(blocks)
    return jnp.transpose(arrived, (1, 0, 2)).reshape(width // n, n * rows)


def per_device(amplitudes, factors, occ_energy, vir_energy, occ_irrep, vir_irrep, pair_orbitals):
    local_pairs = amplitudes.shape[0]
    row_count = amplitudes.shape[1]
    occ_total = occ_energy.shape[0]
    occ_devices = lax.axis_size("occ")
    vir_devices = lax.axis_size("vir")
    occ_index = lax.axis_index("occ")
    vir_index = lax.axis_index("vir")
    lower_half = occ_index < occ_devices // 2

    own = jnp.where(lower_half, amplitudes[0], amplitudes[1])
    outgoing = jnp.where(lower_half, amplitudes[1], amplitudes[0])
    other = passed_along(outgoing, "occ", occ_devices // 2)

    def gather_rows(block):
        spread = jnp.broadcast_to(block[None], (vir_devices,) + block.shape)
        pieces = lax.all_to_all(spread, "vir", split_axis=0, concat_axis=0, tiled=True)
        return pieces.reshape(vir_devices * row_count, block.shape[-1])

    def half_products(rows):
        product = jnp.einsum("cd,qbd->qbc", rows, factors, preferred_element_type=jnp.float32)
        return product.astype(jnp.bfloat16)

    halves_first = half_products(gather_rows(own))
    halves_second = half_products(gather_rows(other))
    direct = jnp.einsum("qac,qbc->ab", factors, halves_first, preferred_element_type=jnp.float32)
    turned_term = jnp.einsum("qac,qbc->ab", halves_second, factors, preferred_element_type=jnp.float32)
    combined = direct + turned_term
    blocks = combined.reshape(vir_devices, row_count, combined.shape[-1]).astype(jnp.bfloat16)
    arrived = lax.all_to_all(blocks, "vir", split_axis=0, concat_axis=0, tiled=True)
    own_rows = jnp.sum(arrived.astype(jnp.float32), axis=0)
    partner_cols = partner_transpose(own_rows, "vir")
    first_out = jnp.where(lower_half, own_rows, partner_cols)
    second_out = jnp.where(lower_half, partner_cols, own_rows)
    summed_pair = jnp.stack([first_out, second_out], axis=0)

    pair_ids = lax.dynamic_slice_in_dim(pair_orbitals, occ_index * local_pairs, local_pairs, 0)
    row_start = vir_index * row_count
    energy_rows = lax.dynamic_slice_in_dim(vir_energy, row_start, row_count, 0)
    irrep_rows = lax.dynamic_slice_in_dim(vir_irrep, row_start, row_count, 0)
    positions = jnp.arange(occ_total, dtype=jnp.int32)
    first_hot = positions[None, :] == pair_ids[:, 0:1]
    second_hot = positions[None, :] == pair_ids[:, 1:2]
    pair_energy = jnp.sum(jnp.where(first_hot, occ_energy[None, :], 0.0), axis=1) + jnp.sum(
        jnp.where(second_hot, occ_energy[None, :], 0.0), axis=1
    )
    first_irrep = jnp.sum(jnp.where(first_hot, occ_irrep[None, :], 0), axis=1)
    second_irrep = jnp.sum(jnp.where(second_hot, occ_irrep[None, :], 0), axis=1)
    pair_sym = jnp.bitwise_xor(first_irrep, second_irrep)
    combined_sym = jnp.bitwise_xor(
        jnp.bitwise_xor(pair_sym[:, None, None], irrep_rows[None, :, None]),
        vir_irrep[None, None, :],
    )
    allowed = combined_sym == 0
    denominator = (
        energy_rows[None, :, None] + vir_energy[None, None, :] - pair_energy[:, None, None]
    )
    return jnp.where(allowed, summed_pair / denominator, jnp.float32(0.0))


def solution(mesh):
    return jax.shard_map(
        per_device,
        mesh=mesh,
        in_specs=(P("occ", "vir", None), P("vir", None, None), P(), P(), P(), P(), P()),
        out_specs=P("occ", "vir", None),
        check_vma=False,
    )
```

```python
import functools

import jax
import jax.numpy as jnp
from jax import lax
from jax.sharding import PartitionSpec as P
from jax.experimental import pallas as pl
from jax.experimental.pallas import tpu as pltpu


def passed_along(block, axis, distance):
    devices = range(lax.axis_size(axis))
    route = [((i - distance) % len(devices), i) for i in devices]
    return lax.ppermute(block, axis, route)


def _exchange_kernel(layout, *refs):
    count = len(layout)
    sources, targets = refs[:count], refs[count:2 * count]
    send_sems, recv_sems = refs[2 * count:3 * count], refs[3 * count:4 * count]
    local_sems = refs[4 * count]
    me = lax.axis_index("vir")
    group = lax.axis_index("occ")

    def peer_of(mine, coord, stride):
        return me + (coord - mine) * stride

    barrier = pltpu.get_barrier_semaphore()
    greetings = 0
    coords = []
    for stride, size, shared in layout:
        mine = lax.rem(lax.div(me, stride), size)
        coords.append(mine)
        for step in range(1, size):
            coord = lax.rem(mine + step, size)
            pl.semaphore_signal(
                barrier, inc=1, device_id=(group, peer_of(mine, coord, stride)),
                device_id_type=pl.DeviceIdType.MESH,
            )
            greetings += 1
    pl.semaphore_wait(barrier, greetings)

    def remote(part, coord, slot):
        stride, size, shared = layout[part]
        mine = coords[part]
        source = sources[part] if shared else sources[part].at[coord]
        return pltpu.make_async_remote_copy(
            src_ref=source,
            dst_ref=targets[part].at[slot],
            send_sem=send_sems[part].at[coord],
            recv_sem=recv_sems[part].at[slot],
            device_id=(group, peer_of(mine, coord, stride)),
            device_id_type=pl.DeviceIdType.MESH,
        )

    locals_ = []
    for part, (stride, size, shared) in enumerate(layout):
        mine = coords[part]
        source = sources[part] if shared else sources[part].at[mine]
        local = pltpu.make_async_copy(source, targets[part].at[mine], local_sems.at[part])
        local.start()
        locals_.append(local)
        for step in range(1, size):
            remote(part, lax.rem(mine + step, size), mine).start()
    for part, (stride, size, shared) in enumerate(layout):
        mine = coords[part]
        for step in range(1, size):
            remote(part, lax.rem(mine + step, size), mine).wait_send()
            origin = lax.rem(mine + size - step, size)
            stride_ = stride
            pltpu.make_async_remote_copy(
                src_ref=sources[part] if shared else sources[part].at[origin],
                dst_ref=targets[part].at[origin],
                send_sem=send_sems[part].at[origin],
                recv_sem=recv_sems[part].at[origin],
                device_id=(group, peer_of(mine, origin, stride_)),
                device_id_type=pl.DeviceIdType.MESH,
            ).wait_recv()
        locals_[part].wait()


def exchange(parts, collective_id):
    layout = tuple((stride, size, shared) for _, stride, size, shared in parts)
    shapes = []
    for array, stride, size, shared in parts:
        block = array.shape if shared else array.shape[1:]
        shapes.append(jax.ShapeDtypeStruct((size,) + tuple(block), array.dtype))
    scratch = [pltpu.SemaphoreType.DMA((size,)) for _, _, size, _ in parts]
    scratch += [pltpu.SemaphoreType.DMA((size,)) for _, _, size, _ in parts]
    scratch.append(pltpu.SemaphoreType.DMA((len(parts),)))
    return pl.pallas_call(
        functools.partial(_exchange_kernel, layout),
        out_shape=tuple(shapes),
        in_specs=[pl.BlockSpec(memory_space=pl.ANY)] * len(parts),
        out_specs=tuple(pl.BlockSpec(memory_space=pl.ANY) for _ in parts),
        scratch_shapes=scratch,
        compiler_params=pltpu.CompilerParams(collective_id=collective_id, has_side_effects=True),
    )(*[array for array, _, _, _ in parts])


def _turn_kernel(n, blocks_ref, out_ref, send_sems, recv_sems):
    me = lax.axis_index("vir")
    group = lax.axis_index("occ")
    partner = lax.rem(group + lax.axis_size("occ") // 2, lax.axis_size("occ"))

    barrier = pltpu.get_barrier_semaphore()

    def greet(k, carry):
        pl.semaphore_signal(barrier, inc=1, device_id=(partner, k), device_id_type=pl.DeviceIdType.MESH)
        return carry

    lax.fori_loop(0, n, greet, 0)
    pl.semaphore_wait(barrier, n)

    def copy_to(k):
        dest = lax.rem(me + k, n)
        return pltpu.make_async_remote_copy(
            src_ref=blocks_ref.at[dest],
            dst_ref=out_ref.at[me],
            send_sem=send_sems.at[dest],
            recv_sem=recv_sems.at[me],
            device_id=(partner, dest),
            device_id_type=pl.DeviceIdType.MESH,
        )

    def send(k, carry):
        copy_to(k).start()
        return carry

    lax.fori_loop(0, n, send, 0)

    def finish(k, carry):
        copy_to(k).wait_send()
        source = lax.rem(me + n - k, n)
        pltpu.make_async_remote_copy(
            src_ref=blocks_ref.at[source],
            dst_ref=out_ref.at[source],
            send_sem=send_sems.at[source],
            recv_sem=recv_sems.at[source],
            device_id=(partner, source),
            device_id_type=pl.DeviceIdType.MESH,
        ).wait_recv()
        return carry

    lax.fori_loop(0, n, finish, 0)


def partner_transpose(own_rows, vir_axis):
    n = lax.axis_size(vir_axis)
    rows, width = own_rows.shape
    blocks = jnp.transpose(own_rows.reshape(rows, n, width // n), (1, 2, 0))
    arrived = pl.pallas_call(
        functools.partial(_turn_kernel, n),
        out_shape=jax.ShapeDtypeStruct(blocks.shape, blocks.dtype),
        in_specs=[pl.BlockSpec(memory_space=pl.ANY)],
        out_specs=pl.BlockSpec(memory_space=pl.ANY),
        scratch_shapes=[pltpu.SemaphoreType.DMA((n,)), pltpu.SemaphoreType.DMA((n,))],
        compiler_params=pltpu.CompilerParams(collective_id=1, has_side_effects=True),
    )(blocks)
    return jnp.transpose(arrived, (1, 0, 2)).reshape(width // n, n * rows)


def per_device(amplitudes, factors, occ_energy, vir_energy, occ_irrep, vir_irrep, pair_orbitals):
    local_pairs = amplitudes.shape[0]
    row_count = amplitudes.shape[1]
    occ_total = occ_energy.shape[0]
    occ_devices = lax.axis_size("occ")
    vir_devices = lax.axis_size("vir")
    occ_index = lax.axis_index("occ")
    vir_index = lax.axis_index("vir")
    lower_half = occ_index < occ_devices // 2

    own = jnp.where(lower_half, amplitudes[0], amplitudes[1])
    outgoing = jnp.where(lower_half, amplitudes[1], amplitudes[0])
    other = passed_along(outgoing, "occ", occ_devices // 2)
    own, other = lax.optimization_barrier((own, other))

    def gather_rows(block):
        spread = jnp.broadcast_to(block[None], (vir_devices,) + block.shape)
        pieces = lax.all_to_all(spread, "vir", split_axis=0, concat_axis=0, tiled=True)
        return pieces.reshape(vir_devices * row_count, block.shape[-1])

    def half_products(rows):
        product = jnp.einsum("cd,qbd->qbc", rows, factors, preferred_element_type=jnp.float32)
        return product.astype(jnp.bfloat16)

    (pieces,) = exchange([(own, 1, vir_devices, True)], 0)
    halves_first = half_products(pieces.reshape(vir_devices * row_count, own.shape[-1]))
    halves_second = half_products(gather_rows(other))
    direct = jnp.einsum("qac,qbc->ab", factors, halves_first, preferred_element_type=jnp.float32)
    turned_term = jnp.einsum("qac,qbc->ab", halves_second, factors, preferred_element_type=jnp.float32)
    combined = direct + turned_term
    blocks = combined.reshape(vir_devices, row_count, combined.shape[-1]).astype(jnp.bfloat16)
    arrived = lax.all_to_all(blocks, "vir", split_axis=0, concat_axis=0, tiled=True)
    own_rows = jnp.sum(arrived.astype(jnp.float32), axis=0)
    partner_cols = partner_transpose(own_rows, "vir")
    first_out = jnp.where(lower_half, own_rows, partner_cols)
    second_out = jnp.where(lower_half, partner_cols, own_rows)
    summed_pair = jnp.stack([first_out, second_out], axis=0)

    pair_ids = lax.dynamic_slice_in_dim(pair_orbitals, occ_index * local_pairs, local_pairs, 0)
    row_start = vir_index * row_count
    energy_rows = lax.dynamic_slice_in_dim(vir_energy, row_start, row_count, 0)
    irrep_rows = lax.dynamic_slice_in_dim(vir_irrep, row_start, row_count, 0)
    positions = jnp.arange(occ_total, dtype=jnp.int32)
    first_hot = positions[None, :] == pair_ids[:, 0:1]
    second_hot = positions[None, :] == pair_ids[:, 1:2]
    pair_energy = jnp.sum(jnp.where(first_hot, occ_energy[None, :], 0.0), axis=1) + jnp.sum(
        jnp.where(second_hot, occ_energy[None, :], 0.0), axis=1
    )
    first_irrep = jnp.sum(jnp.where(first_hot, occ_irrep[None, :], 0), axis=1)
    second_irrep = jnp.sum(jnp.where(second_hot, occ_irrep[None, :], 0), axis=1)
    pair_sym = jnp.bitwise_xor(first_irrep, second_irrep)
    combined_sym = jnp.bitwise_xor(
        jnp.bitwise_xor(pair_sym[:, None, None], irrep_rows[None, :, None]),
        vir_irrep[None, None, :],
    )
    allowed = combined_sym == 0
    denominator = (
        energy_rows[None, :, None] + vir_energy[None, None, :] - pair_energy[:, None, None]
    )
    return jnp.where(allowed, summed_pair / denominator, jnp.float32(0.0))


def solution(mesh):
    return jax.shard_map(
        per_device,
        mesh=mesh,
        in_specs=(P("occ", "vir", None), P("vir", None, None), P(), P(), P(), P(), P()),
        out_specs=P("occ", "vir", None),
        check_vma=False,
    )
```

```python
import functools

import jax
import jax.numpy as jnp
from jax import lax
from jax.sharding import PartitionSpec as P
from jax.experimental import pallas as pl
from jax.experimental.pallas import tpu as pltpu


def passed_along(block, axis, distance):
    devices = range(lax.axis_size(axis))
    route = [((i - distance) % len(devices), i) for i in devices]
    return lax.ppermute(block, axis, route)


def _turn_kernel(n, rows_ref, out_ref, flipped, send_sems, recv_sems):
    me = lax.axis_index("vir")
    rows = rows_ref.shape[0]
    flipped[...] = jnp.transpose(rows_ref[...], (1, 0))
    group = lax.axis_index("occ")
    partner = lax.rem(group + lax.axis_size("occ") // 2, lax.axis_size("occ"))

    barrier = pltpu.get_barrier_semaphore()

    def greet(k, carry):
        pl.semaphore_signal(barrier, inc=1, device_id=(partner, k), device_id_type=pl.DeviceIdType.MESH)
        return carry

    lax.fori_loop(0, n, greet, 0)
    pl.semaphore_wait(barrier, n)

    def copy_to(k):
        dest = lax.rem(me + k, n)
        return pltpu.make_async_remote_copy(
            src_ref=flipped.at[pl.ds(pl.multiple_of(dest * rows, rows), rows)],
            dst_ref=out_ref.at[me],
            send_sem=send_sems.at[dest],
            recv_sem=recv_sems.at[me],
            device_id=(partner, dest),
            device_id_type=pl.DeviceIdType.MESH,
        )

    def send(k, carry):
        copy_to(k).start()
        return carry

    lax.fori_loop(0, n, send, 0)

    def finish(k, carry):
        copy_to(k).wait_send()
        source = lax.rem(me + n - k, n)
        pltpu.make_async_remote_copy(
            src_ref=flipped.at[pl.ds(pl.multiple_of(source * rows, rows), rows)],
            dst_ref=out_ref.at[source],
            send_sem=send_sems.at[source],
            recv_sem=recv_sems.at[source],
            device_id=(partner, source),
            device_id_type=pl.DeviceIdType.MESH,
        ).wait_recv()
        return carry

    lax.fori_loop(0, n, finish, 0)


def partner_transpose(own_rows, vir_axis):
    n = lax.axis_size(vir_axis)
    rows, width = own_rows.shape
    arrived = pl.pallas_call(
        functools.partial(_turn_kernel, n),
        out_shape=jax.ShapeDtypeStruct((n, rows, rows), own_rows.dtype),
        in_specs=[pl.BlockSpec(memory_space=pltpu.VMEM)],
        out_specs=pl.BlockSpec(memory_space=pl.ANY),
        scratch_shapes=[
            pltpu.VMEM((width, rows), own_rows.dtype),
            pltpu.SemaphoreType.DMA((n,)),
            pltpu.SemaphoreType.DMA((n,)),
        ],
        compiler_params=pltpu.CompilerParams(collective_id=1, has_side_effects=True),
    )(own_rows)
    return jnp.transpose(arrived, (1, 0, 2)).reshape(width // n, n * rows)


def per_device(amplitudes, factors, occ_energy, vir_energy, occ_irrep, vir_irrep, pair_orbitals):
    local_pairs = amplitudes.shape[0]
    row_count = amplitudes.shape[1]
    occ_total = occ_energy.shape[0]
    occ_devices = lax.axis_size("occ")
    vir_devices = lax.axis_size("vir")
    occ_index = lax.axis_index("occ")
    vir_index = lax.axis_index("vir")
    lower_half = occ_index < occ_devices // 2

    own = jnp.where(lower_half, amplitudes[0], amplitudes[1])
    outgoing = jnp.where(lower_half, amplitudes[1], amplitudes[0])
    other = passed_along(outgoing, "occ", occ_devices // 2)
    own, other = lax.optimization_barrier((own, other))

    def gather_rows(block):
        spread = jnp.broadcast_to(block[None], (vir_devices,) + block.shape)
        pieces = lax.all_to_all(spread, "vir", split_axis=0, concat_axis=0, tiled=True)
        return pieces.reshape(vir_devices * row_count, block.shape[-1])

    def half_products(rows):
        product = jnp.einsum("cd,qbd->qbc", rows, factors, preferred_element_type=jnp.float32)
        return product.astype(jnp.bfloat16)

    halves_first = half_products(gather_rows(own))
    halves_second = half_products(gather_rows(other))
    direct = jnp.einsum("qac,qbc->ab", factors, halves_first, preferred_element_type=jnp.float32)
    turned_term = jnp.einsum("qac,qbc->ab", halves_second, factors, preferred_element_type=jnp.float32)
    combined = direct + turned_term
    blocks = combined.reshape(vir_devices, row_count, combined.shape[-1]).astype(jnp.bfloat16)
    arrived = lax.all_to_all(blocks, "vir", split_axis=0, concat_axis=0, tiled=True)
    own_rows = jnp.sum(arrived.astype(jnp.float32), axis=0)
    partner_cols = partner_transpose(own_rows, "vir")
    first_out = jnp.where(lower_half, own_rows, partner_cols)
    second_out = jnp.where(lower_half, partner_cols, own_rows)
    summed_pair = jnp.stack([first_out, second_out], axis=0)

    pair_ids = lax.dynamic_slice_in_dim(pair_orbitals, occ_index * local_pairs, local_pairs, 0)
    row_start = vir_index * row_count
    energy_rows = lax.dynamic_slice_in_dim(vir_energy, row_start, row_count, 0)
    irrep_rows = lax.dynamic_slice_in_dim(vir_irrep, row_start, row_count, 0)
    positions = jnp.arange(occ_total, dtype=jnp.int32)
    first_hot = positions[None, :] == pair_ids[:, 0:1]
    second_hot = positions[None, :] == pair_ids[:, 1:2]
    pair_energy = jnp.sum(jnp.where(first_hot, occ_energy[None, :], 0.0), axis=1) + jnp.sum(
        jnp.where(second_hot, occ_energy[None, :], 0.0), axis=1
    )
    first_irrep = jnp.sum(jnp.where(first_hot, occ_irrep[None, :], 0), axis=1)
    second_irrep = jnp.sum(jnp.where(second_hot, occ_irrep[None, :], 0), axis=1)
    pair_sym = jnp.bitwise_xor(first_irrep, second_irrep)
    combined_sym = jnp.bitwise_xor(
        jnp.bitwise_xor(pair_sym[:, None, None], irrep_rows[None, :, None]),
        vir_irrep[None, None, :],
    )
    allowed = combined_sym == 0
    denominator = (
        energy_rows[None, :, None] + vir_energy[None, None, :] - pair_energy[:, None, None]
    )
    return jnp.where(allowed, summed_pair / denominator, jnp.float32(0.0))


def solution(mesh):
    return jax.shard_map(
        per_device,
        mesh=mesh,
        in_specs=(P("occ", "vir", None), P("vir", None, None), P(), P(), P(), P(), P()),
        out_specs=P("occ", "vir", None),
        check_vma=False,
    )
```

```python
import functools

import jax
import jax.numpy as jnp
from jax import lax
from jax.sharding import PartitionSpec as P
from jax.experimental import pallas as pl
from jax.experimental.pallas import tpu as pltpu


def passed_along(block, axis, distance):
    devices = range(lax.axis_size(axis))
    route = [((i - distance) % len(devices), i) for i in devices]
    return lax.ppermute(block, axis, route)


def _turned_scatter_kernel(n, groups, factors_ref, other_ref, direct_ref, out_ref, hbuf, cbuf, send_sems, recv_sems, own_sem):
    me = lax.axis_index("vir")
    group = lax.axis_index("occ")
    q_count = factors_ref.shape[0]
    rows = out_ref.shape[1]
    width = out_ref.shape[2]
    per_group = n // groups
    span = per_group * rows
    tile = min(256, width)
    tiles = width // tile
    dims = (((1,), (1,)), ((), ()))

    barrier = pltpu.get_barrier_semaphore()

    def greet(k, carry):
        pl.semaphore_signal(
            barrier, inc=1, device_id=(group, lax.rem(me + k, n)), device_id_type=pl.DeviceIdType.MESH
        )
        return carry

    lax.fori_loop(1, n, greet, 0)
    pl.semaphore_wait(barrier, n - 1)

    def remote(slot, i, dest):
        return pltpu.make_async_remote_copy(
            src_ref=cbuf.at[slot, pl.ds(i * rows, rows)],
            dst_ref=out_ref.at[me],
            send_sem=send_sems.at[dest],
            recv_sem=recv_sems.at[me],
            device_id=(group, dest),
            device_id_type=pl.DeviceIdType.MESH,
        )

    def local(slot, i):
        return pltpu.make_async_copy(cbuf.at[slot, pl.ds(i * rows, rows)], out_ref.at[me], own_sem)

    def group_at(step):
        return lax.rem(me // per_group + 1 + step, groups)

    def settle(step):
        slot = step % 2
        chosen = group_at(step)
        for i in range(per_group):
            dest = chosen * per_group + i

            @pl.when(dest != me)
            def _():
                remote(slot, i, dest).wait_send()

            @pl.when(dest == me)
            def _():
                local(slot, i).wait()

    for step in range(groups):
        slot = step % 2
        if step >= 2:
            settle(step - 2)
        chosen = group_at(step)
        row0 = pl.multiple_of(chosen * span, span)

        def halves(t, carry):
            col0 = pl.multiple_of(t * tile, tile)
            for q in range(q_count):
                product = lax.dot_general(
                    factors_ref[q, pl.ds(row0, span), :], other_ref[pl.ds(col0, tile), :],
                    dims, preferred_element_type=jnp.float32,
                )
                hbuf[q, :, pl.ds(col0, tile)] = product.astype(hbuf.dtype)
            return carry

        lax.fori_loop(0, tiles, halves, 0)

        def product(t, carry):
            col0 = pl.multiple_of(t * tile, tile)
            acc = direct_ref[pl.ds(row0, span), pl.ds(col0, tile)]
            for q in range(q_count):
                acc += lax.dot_general(
                    hbuf[q], factors_ref[q, pl.ds(col0, tile), :],
                    dims, preferred_element_type=jnp.float32,
                )
            cbuf[slot, :, pl.ds(col0, tile)] = acc.astype(cbuf.dtype)
            return carry

        lax.fori_loop(0, tiles, product, 0)
        for i in range(per_group):
            dest = chosen * per_group + i

            @pl.when(dest != me)
            def _():
                remote(slot, i, dest).start()

            @pl.when(dest == me)
            def _():
                local(slot, i).start()

    for step in range(max(groups - 2, 0), groups):
        settle(step)

    def arrive(k, carry):
        source = lax.rem(me + k, n)
        pltpu.make_async_remote_copy(
            src_ref=cbuf.at[0, pl.ds(0, rows)],
            dst_ref=out_ref.at[source],
            send_sem=send_sems.at[source],
            recv_sem=recv_sems.at[source],
            device_id=(group, source),
            device_id_type=pl.DeviceIdType.MESH,
        ).wait_recv()
        return carry

    lax.fori_loop(1, n, arrive, 0)


def turned_rows(factors, other_rows, direct, vir_axis):
    n = lax.axis_size(vir_axis)
    width = factors.shape[1]
    rows = width // n
    groups = 4
    span = (n // groups) * rows
    arrived = pl.pallas_call(
        functools.partial(_turned_scatter_kernel, n, groups),
        out_shape=jax.ShapeDtypeStruct((n, rows, width), jnp.bfloat16),
        in_specs=[pl.BlockSpec(memory_space=pltpu.VMEM)] * 3,
        out_specs=pl.BlockSpec(memory_space=pl.ANY),
        scratch_shapes=[
            pltpu.VMEM((factors.shape[0], span, width), jnp.bfloat16),
            pltpu.VMEM((2, span, width), jnp.bfloat16),
            pltpu.SemaphoreType.DMA((n,)),
            pltpu.SemaphoreType.DMA((n,)),
            pltpu.SemaphoreType.DMA,
        ],
        compiler_params=pltpu.CompilerParams(
            collective_id=0, has_side_effects=True, vmem_limit_bytes=48 * 1024 * 1024
        ),
    )(factors, other_rows, direct)
    return jnp.sum(arrived.astype(jnp.float32), axis=0)


def _turn_kernel(n, blocks_ref, out_ref, send_sems, recv_sems):
    me = lax.axis_index("vir")
    group = lax.axis_index("occ")
    partner = lax.rem(group + lax.axis_size("occ") // 2, lax.axis_size("occ"))

    barrier = pltpu.get_barrier_semaphore()

    def greet(k, carry):
        pl.semaphore_signal(barrier, inc=1, device_id=(partner, k), device_id_type=pl.DeviceIdType.MESH)
        return carry

    lax.fori_loop(0, n, greet, 0)
    pl.semaphore_wait(barrier, n)

    def copy_to(k):
        dest = lax.rem(me + k, n)
        return pltpu.make_async_remote_copy(
            src_ref=blocks_ref.at[dest],
            dst_ref=out_ref.at[me],
            send_sem=send_sems.at[dest],
            recv_sem=recv_sems.at[me],
            device_id=(partner, dest),
            device_id_type=pl.DeviceIdType.MESH,
        )

    def send(k, carry):
        copy_to(k).start()
        return carry

    lax.fori_loop(0, n, send, 0)

    def finish(k, carry):
        copy_to(k).wait_send()
        source = lax.rem(me + n - k, n)
        pltpu.make_async_remote_copy(
            src_ref=blocks_ref.at[source],
            dst_ref=out_ref.at[source],
            send_sem=send_sems.at[source],
            recv_sem=recv_sems.at[source],
            device_id=(partner, source),
            device_id_type=pl.DeviceIdType.MESH,
        ).wait_recv()
        return carry

    lax.fori_loop(0, n, finish, 0)


def partner_transpose(own_rows, vir_axis):
    n = lax.axis_size(vir_axis)
    rows, width = own_rows.shape
    blocks = jnp.transpose(own_rows.reshape(rows, n, width // n), (1, 2, 0))
    arrived = pl.pallas_call(
        functools.partial(_turn_kernel, n),
        out_shape=jax.ShapeDtypeStruct(blocks.shape, blocks.dtype),
        in_specs=[pl.BlockSpec(memory_space=pl.ANY)],
        out_specs=pl.BlockSpec(memory_space=pl.ANY),
        scratch_shapes=[pltpu.SemaphoreType.DMA((n,)), pltpu.SemaphoreType.DMA((n,))],
        compiler_params=pltpu.CompilerParams(collective_id=1, has_side_effects=True),
    )(blocks)
    return jnp.transpose(arrived, (1, 0, 2)).reshape(width // n, n * rows)


def per_device(amplitudes, factors, occ_energy, vir_energy, occ_irrep, vir_irrep, pair_orbitals):
    local_pairs = amplitudes.shape[0]
    row_count = amplitudes.shape[1]
    occ_total = occ_energy.shape[0]
    occ_devices = lax.axis_size("occ")
    vir_devices = lax.axis_size("vir")
    occ_index = lax.axis_index("occ")
    vir_index = lax.axis_index("vir")
    lower_half = occ_index < occ_devices // 2

    own = jnp.where(lower_half, amplitudes[0], amplitudes[1])
    outgoing = jnp.where(lower_half, amplitudes[1], amplitudes[0])
    other = passed_along(outgoing, "occ", occ_devices // 2)
    own, other = lax.optimization_barrier((own, other))

    def gather_rows(block):
        spread = jnp.broadcast_to(block[None], (vir_devices,) + block.shape)
        pieces = lax.all_to_all(spread, "vir", split_axis=0, concat_axis=0, tiled=True)
        return pieces.reshape(vir_devices * row_count, block.shape[-1])

    def half_products(rows):
        product = jnp.einsum("cd,qbd->qbc", rows, factors, preferred_element_type=jnp.float32)
        return product.astype(jnp.bfloat16)

    halves_first = half_products(gather_rows(own))
    direct = jnp.einsum("qac,qbc->ab", factors, halves_first, preferred_element_type=jnp.float32)
    own_rows = turned_rows(factors, gather_rows(other), direct, "vir")
    partner_cols = partner_transpose(own_rows, "vir")
    first_out = jnp.where(lower_half, own_rows, partner_cols)
    second_out = jnp.where(lower_half, partner_cols, own_rows)
    summed_pair = jnp.stack([first_out, second_out], axis=0)

    pair_ids = lax.dynamic_slice_in_dim(pair_orbitals, occ_index * local_pairs, local_pairs, 0)
    row_start = vir_index * row_count
    energy_rows = lax.dynamic_slice_in_dim(vir_energy, row_start, row_count, 0)
    irrep_rows = lax.dynamic_slice_in_dim(vir_irrep, row_start, row_count, 0)
    positions = jnp.arange(occ_total, dtype=jnp.int32)
    first_hot = positions[None, :] == pair_ids[:, 0:1]
    second_hot = positions[None, :] == pair_ids[:, 1:2]
    pair_energy = jnp.sum(jnp.where(first_hot, occ_energy[None, :], 0.0), axis=1) + jnp.sum(
        jnp.where(second_hot, occ_energy[None, :], 0.0), axis=1
    )
    first_irrep = jnp.sum(jnp.where(first_hot, occ_irrep[None, :], 0), axis=1)
    second_irrep = jnp.sum(jnp.where(second_hot, occ_irrep[None, :], 0), axis=1)
    pair_sym = jnp.bitwise_xor(first_irrep, second_irrep)
    combined_sym = jnp.bitwise_xor(
        jnp.bitwise_xor(pair_sym[:, None, None], irrep_rows[None, :, None]),
        vir_irrep[None, None, :],
    )
    allowed = combined_sym == 0
    denominator = (
        energy_rows[None, :, None] + vir_energy[None, None, :] - pair_energy[:, None, None]
    )
    return jnp.where(allowed, summed_pair / denominator, jnp.float32(0.0))


def solution(mesh):
    return jax.shard_map(
        per_device,
        mesh=mesh,
        in_specs=(P("occ", "vir", None), P("vir", None, None), P(), P(), P(), P(), P()),
        out_specs=P("occ", "vir", None),
        check_vma=False,
    )
```

```python
import functools

import jax
import jax.numpy as jnp
from jax import lax
from jax.sharding import PartitionSpec as P
from jax.experimental import pallas as pl
from jax.experimental.pallas import tpu as pltpu


def passed_along(block, axis, distance):
    devices = range(lax.axis_size(axis))
    route = [((i - distance) % len(devices), i) for i in devices]
    return lax.ppermute(block, axis, route)


def _turned_scatter_kernel(n, groups, factors_ref, other_ref, direct_ref, out_ref, hbuf, cbuf, send_sems, recv_sems, own_sem):
    me = lax.axis_index("vir")
    group = lax.axis_index("occ")
    q_count = factors_ref.shape[0]
    rows = out_ref.shape[1]
    width = out_ref.shape[2]
    per_group = n // groups
    span = per_group * rows
    tile = min(256, width)
    tiles = width // tile
    dims = (((1,), (1,)), ((), ()))

    barrier = pltpu.get_barrier_semaphore()

    def greet(k, carry):
        pl.semaphore_signal(
            barrier, inc=1, device_id=(group, lax.rem(me + k, n)), device_id_type=pl.DeviceIdType.MESH
        )
        return carry

    lax.fori_loop(1, n, greet, 0)
    pl.semaphore_wait(barrier, n - 1)

    def remote(slot, i, dest):
        return pltpu.make_async_remote_copy(
            src_ref=cbuf.at[slot, pl.ds(i * rows, rows)],
            dst_ref=out_ref.at[me],
            send_sem=send_sems.at[dest],
            recv_sem=recv_sems.at[me],
            device_id=(group, dest),
            device_id_type=pl.DeviceIdType.MESH,
        )

    def local(slot, i):
        return pltpu.make_async_copy(cbuf.at[slot, pl.ds(i * rows, rows)], out_ref.at[me], own_sem)

    def group_at(step):
        return lax.rem(me // per_group + 1 + step, groups)

    def settle(step):
        slot = step % 2
        chosen = group_at(step)
        for i in range(per_group):
            dest = chosen * per_group + i

            @pl.when(dest != me)
            def _():
                remote(slot, i, dest).wait_send()

            @pl.when(dest == me)
            def _():
                local(slot, i).wait()

    for step in range(groups):
        slot = step % 2
        if step >= 2:
            settle(step - 2)
        chosen = group_at(step)
        row0 = pl.multiple_of(chosen * span, span)

        def halves(t, carry):
            col0 = pl.multiple_of(t * tile, tile)
            for q in range(q_count):
                product = lax.dot_general(
                    factors_ref[q, pl.ds(row0, span), :], other_ref[pl.ds(col0, tile), :],
                    dims, preferred_element_type=jnp.float32,
                )
                hbuf[q, :, pl.ds(col0, tile)] = product.astype(hbuf.dtype)
            return carry

        lax.fori_loop(0, tiles, halves, 0)

        def product(t, carry):
            col0 = pl.multiple_of(t * tile, tile)
            acc = direct_ref[pl.ds(row0, span), pl.ds(col0, tile)]
            for q in range(q_count):
                acc += lax.dot_general(
                    hbuf[q], factors_ref[q, pl.ds(col0, tile), :],
                    dims, preferred_element_type=jnp.float32,
                )
            cbuf[slot, :, pl.ds(col0, tile)] = acc.astype(cbuf.dtype)
            return carry

        lax.fori_loop(0, tiles, product, 0)
        for i in range(per_group):
            dest = chosen * per_group + i

            @pl.when(dest != me)
            def _():
                remote(slot, i, dest).start()

            @pl.when(dest == me)
            def _():
                local(slot, i).start()

    for step in range(max(groups - 2, 0), groups):
        settle(step)

    def arrive(k, carry):
        source = lax.rem(me + k, n)
        pltpu.make_async_remote_copy(
            src_ref=cbuf.at[0, pl.ds(0, rows)],
            dst_ref=out_ref.at[source],
            send_sem=send_sems.at[source],
            recv_sem=recv_sems.at[source],
            device_id=(group, source),
            device_id_type=pl.DeviceIdType.MESH,
        ).wait_recv()
        return carry

    lax.fori_loop(1, n, arrive, 0)


def turned_rows(factors, other_rows, direct, vir_axis):
    n = lax.axis_size(vir_axis)
    width = factors.shape[1]
    rows = width // n
    groups = 8
    span = (n // groups) * rows
    arrived = pl.pallas_call(
        functools.partial(_turned_scatter_kernel, n, groups),
        out_shape=jax.ShapeDtypeStruct((n, rows, width), jnp.bfloat16),
        in_specs=[pl.BlockSpec(memory_space=pltpu.VMEM)] * 3,
        out_specs=pl.BlockSpec(memory_space=pl.ANY),
        scratch_shapes=[
            pltpu.VMEM((factors.shape[0], span, width), jnp.bfloat16),
            pltpu.VMEM((2, span, width), jnp.bfloat16),
            pltpu.SemaphoreType.DMA((n,)),
            pltpu.SemaphoreType.DMA((n,)),
            pltpu.SemaphoreType.DMA,
        ],
        compiler_params=pltpu.CompilerParams(
            collective_id=0, has_side_effects=True, vmem_limit_bytes=48 * 1024 * 1024
        ),
    )(factors, other_rows, direct)
    return jnp.sum(arrived.astype(jnp.float32), axis=0)


def _turn_kernel(n, blocks_ref, out_ref, send_sems, recv_sems):
    me = lax.axis_index("vir")
    group = lax.axis_index("occ")
    partner = lax.rem(group + lax.axis_size("occ") // 2, lax.axis_size("occ"))

    barrier = pltpu.get_barrier_semaphore()

    def greet(k, carry):
        pl.semaphore_signal(barrier, inc=1, device_id=(partner, k), device_id_type=pl.DeviceIdType.MESH)
        return carry

    lax.fori_loop(0, n, greet, 0)
    pl.semaphore_wait(barrier, n)

    def copy_to(k):
        dest = lax.rem(me + k, n)
        return pltpu.make_async_remote_copy(
            src_ref=blocks_ref.at[dest],
            dst_ref=out_ref.at[me],
            send_sem=send_sems.at[dest],
            recv_sem=recv_sems.at[me],
            device_id=(partner, dest),
            device_id_type=pl.DeviceIdType.MESH,
        )

    def send(k, carry):
        copy_to(k).start()
        return carry

    lax.fori_loop(0, n, send, 0)

    def finish(k, carry):
        copy_to(k).wait_send()
        source = lax.rem(me + n - k, n)
        pltpu.make_async_remote_copy(
            src_ref=blocks_ref.at[source],
            dst_ref=out_ref.at[source],
            send_sem=send_sems.at[source],
            recv_sem=recv_sems.at[source],
            device_id=(partner, source),
            device_id_type=pl.DeviceIdType.MESH,
        ).wait_recv()
        return carry

    lax.fori_loop(0, n, finish, 0)


def partner_transpose(own_rows, vir_axis):
    n = lax.axis_size(vir_axis)
    rows, width = own_rows.shape
    blocks = jnp.transpose(own_rows.reshape(rows, n, width // n), (1, 2, 0))
    arrived = pl.pallas_call(
        functools.partial(_turn_kernel, n),
        out_shape=jax.ShapeDtypeStruct(blocks.shape, blocks.dtype),
        in_specs=[pl.BlockSpec(memory_space=pl.ANY)],
        out_specs=pl.BlockSpec(memory_space=pl.ANY),
        scratch_shapes=[pltpu.SemaphoreType.DMA((n,)), pltpu.SemaphoreType.DMA((n,))],
        compiler_params=pltpu.CompilerParams(collective_id=1, has_side_effects=True),
    )(blocks)
    return jnp.transpose(arrived, (1, 0, 2)).reshape(width // n, n * rows)


def per_device(amplitudes, factors, occ_energy, vir_energy, occ_irrep, vir_irrep, pair_orbitals):
    local_pairs = amplitudes.shape[0]
    row_count = amplitudes.shape[1]
    occ_total = occ_energy.shape[0]
    occ_devices = lax.axis_size("occ")
    vir_devices = lax.axis_size("vir")
    occ_index = lax.axis_index("occ")
    vir_index = lax.axis_index("vir")
    lower_half = occ_index < occ_devices // 2

    own = jnp.where(lower_half, amplitudes[0], amplitudes[1])
    outgoing = jnp.where(lower_half, amplitudes[1], amplitudes[0])
    other = passed_along(outgoing, "occ", occ_devices // 2)
    own, other = lax.optimization_barrier((own, other))

    def gather_rows(block):
        spread = jnp.broadcast_to(block[None], (vir_devices,) + block.shape)
        pieces = lax.all_to_all(spread, "vir", split_axis=0, concat_axis=0, tiled=True)
        return pieces.reshape(vir_devices * row_count, block.shape[-1])

    def half_products(rows):
        product = jnp.einsum("cd,qbd->qbc", rows, factors, preferred_element_type=jnp.float32)
        return product.astype(jnp.bfloat16)

    halves_first = half_products(gather_rows(own))
    direct = jnp.einsum("qac,qbc->ab", factors, halves_first, preferred_element_type=jnp.float32)
    own_rows = turned_rows(factors, gather_rows(other), direct, "vir")
    partner_cols = partner_transpose(own_rows, "vir")
    first_out = jnp.where(lower_half, own_rows, partner_cols)
    second_out = jnp.where(lower_half, partner_cols, own_rows)
    summed_pair = jnp.stack([first_out, second_out], axis=0)

    pair_ids = lax.dynamic_slice_in_dim(pair_orbitals, occ_index * local_pairs, local_pairs, 0)
    row_start = vir_index * row_count
    energy_rows = lax.dynamic_slice_in_dim(vir_energy, row_start, row_count, 0)
    irrep_rows = lax.dynamic_slice_in_dim(vir_irrep, row_start, row_count, 0)
    positions = jnp.arange(occ_total, dtype=jnp.int32)
    first_hot = positions[None, :] == pair_ids[:, 0:1]
    second_hot = positions[None, :] == pair_ids[:, 1:2]
    pair_energy = jnp.sum(jnp.where(first_hot, occ_energy[None, :], 0.0), axis=1) + jnp.sum(
        jnp.where(second_hot, occ_energy[None, :], 0.0), axis=1
    )
    first_irrep = jnp.sum(jnp.where(first_hot, occ_irrep[None, :], 0), axis=1)
    second_irrep = jnp.sum(jnp.where(second_hot, occ_irrep[None, :], 0), axis=1)
    pair_sym = jnp.bitwise_xor(first_irrep, second_irrep)
    combined_sym = jnp.bitwise_xor(
        jnp.bitwise_xor(pair_sym[:, None, None], irrep_rows[None, :, None]),
        vir_irrep[None, None, :],
    )
    allowed = combined_sym == 0
    denominator = (
        energy_rows[None, :, None] + vir_energy[None, None, :] - pair_energy[:, None, None]
    )
    return jnp.where(allowed, summed_pair / denominator, jnp.float32(0.0))


def solution(mesh):
    return jax.shard_map(
        per_device,
        mesh=mesh,
        in_specs=(P("occ", "vir", None), P("vir", None, None), P(), P(), P(), P(), P()),
        out_specs=P("occ", "vir", None),
        check_vma=False,
    )
```

```python
import functools

import jax
import jax.numpy as jnp
from jax import lax
from jax.sharding import PartitionSpec as P
from jax.experimental import pallas as pl
from jax.experimental.pallas import tpu as pltpu


def passed_along(block, axis, distance):
    devices = range(lax.axis_size(axis))
    route = [((i - distance) % len(devices), i) for i in devices]
    return lax.ppermute(block, axis, route)


def _turned_scatter_kernel(n, groups, factors_ref, flipped_ref, other_ref, direct_ref, out_ref, hbuf, cbuf, send_sems, recv_sems, own_sem):
    me = lax.axis_index("vir")
    group = lax.axis_index("occ")
    q_count = factors_ref.shape[0]
    rows = out_ref.shape[1]
    width = out_ref.shape[2]
    per_group = n // groups
    span = per_group * rows
    tile = min(256, width)
    tiles = width // tile
    dims = (((1,), (1,)), ((), ()))

    barrier = pltpu.get_barrier_semaphore()

    def greet(k, carry):
        pl.semaphore_signal(
            barrier, inc=1, device_id=(group, lax.rem(me + k, n)), device_id_type=pl.DeviceIdType.MESH
        )
        return carry

    lax.fori_loop(1, n, greet, 0)
    pl.semaphore_wait(barrier, n - 1)

    def remote(slot, i, dest):
        return pltpu.make_async_remote_copy(
            src_ref=cbuf.at[slot, pl.ds(i * rows, rows)],
            dst_ref=out_ref.at[me],
            send_sem=send_sems.at[dest],
            recv_sem=recv_sems.at[me],
            device_id=(group, dest),
            device_id_type=pl.DeviceIdType.MESH,
        )

    def local(slot, i):
        return pltpu.make_async_copy(cbuf.at[slot, pl.ds(i * rows, rows)], out_ref.at[me], own_sem)

    def group_at(step):
        return lax.rem(me // per_group + 1 + step, groups)

    def settle(step):
        slot = step % 2
        chosen = group_at(step)
        for i in range(per_group):
            dest = chosen * per_group + i

            @pl.when(dest != me)
            def _():
                remote(slot, i, dest).wait_send()

            @pl.when(dest == me)
            def _():
                local(slot, i).wait()

    for step in range(groups):
        slot = step % 2
        if step >= 2:
            settle(step - 2)
        chosen = group_at(step)
        row0 = pl.multiple_of(chosen * span, span)

        def halves(t, carry):
            col0 = pl.multiple_of(t * tile, tile)
            for q in range(q_count):
                product = jnp.dot(
                    factors_ref[q, pl.ds(row0, span), :], other_ref[:, pl.ds(col0, tile)],
                    preferred_element_type=jnp.float32,
                )
                hbuf[q, :, pl.ds(col0, tile)] = product.astype(hbuf.dtype)
            return carry

        lax.fori_loop(0, tiles, halves, 0)

        def product(t, carry):
            col0 = pl.multiple_of(t * tile, tile)
            acc = direct_ref[pl.ds(row0, span), pl.ds(col0, tile)]
            for q in range(q_count):
                acc += jnp.dot(
                    hbuf[q], flipped_ref[q, :, pl.ds(col0, tile)], preferred_element_type=jnp.float32
                )
            cbuf[slot, :, pl.ds(col0, tile)] = acc.astype(cbuf.dtype)
            return carry

        lax.fori_loop(0, tiles, product, 0)
        for i in range(per_group):
            dest = chosen * per_group + i

            @pl.when(dest != me)
            def _():
                remote(slot, i, dest).start()

            @pl.when(dest == me)
            def _():
                local(slot, i).start()

    for step in range(max(groups - 2, 0), groups):
        settle(step)

    def arrive(k, carry):
        source = lax.rem(me + k, n)
        pltpu.make_async_remote_copy(
            src_ref=cbuf.at[0, pl.ds(0, rows)],
            dst_ref=out_ref.at[source],
            send_sem=send_sems.at[source],
            recv_sem=recv_sems.at[source],
            device_id=(group, source),
            device_id_type=pl.DeviceIdType.MESH,
        ).wait_recv()
        return carry

    lax.fori_loop(1, n, arrive, 0)


def turned_rows(factors, other_rows, direct, vir_axis):
    n = lax.axis_size(vir_axis)
    width = factors.shape[1]
    rows = width // n
    groups = 4
    span = (n // groups) * rows
    arrived = pl.pallas_call(
        functools.partial(_turned_scatter_kernel, n, groups),
        out_shape=jax.ShapeDtypeStruct((n, rows, width), jnp.bfloat16),
        in_specs=[pl.BlockSpec(memory_space=pltpu.VMEM)] * 4,
        out_specs=pl.BlockSpec(memory_space=pl.ANY),
        scratch_shapes=[
            pltpu.VMEM((factors.shape[0], span, width), jnp.bfloat16),
            pltpu.VMEM((2, span, width), jnp.bfloat16),
            pltpu.SemaphoreType.DMA((n,)),
            pltpu.SemaphoreType.DMA((n,)),
            pltpu.SemaphoreType.DMA,
        ],
        compiler_params=pltpu.CompilerParams(
            collective_id=0, has_side_effects=True, vmem_limit_bytes=48 * 1024 * 1024
        ),
    )(factors, jnp.transpose(factors, (0, 2, 1)), jnp.transpose(other_rows, (1, 0)), direct)
    return jnp.sum(arrived.astype(jnp.float32), axis=0)


def _turn_kernel(n, blocks_ref, out_ref, send_sems, recv_sems):
    me = lax.axis_index("vir")
    group = lax.axis_index("occ")
    partner = lax.rem(group + lax.axis_size("occ") // 2, lax.axis_size("occ"))

    barrier = pltpu.get_barrier_semaphore()

    def greet(k, carry):
        pl.semaphore_signal(barrier, inc=1, device_id=(partner, k), device_id_type=pl.DeviceIdType.MESH)
        return carry

    lax.fori_loop(0, n, greet, 0)
    pl.semaphore_wait(barrier, n)

    def copy_to(k):
        dest = lax.rem(me + k, n)
        return pltpu.make_async_remote_copy(
            src_ref=blocks_ref.at[dest],
            dst_ref=out_ref.at[me],
            send_sem=send_sems.at[dest],
            recv_sem=recv_sems.at[me],
            device_id=(partner, dest),
            device_id_type=pl.DeviceIdType.MESH,
        )

    def send(k, carry):
        copy_to(k).start()
        return carry

    lax.fori_loop(0, n, send, 0)

    def finish(k, carry):
        copy_to(k).wait_send()
        source = lax.rem(me + n - k, n)
        pltpu.make_async_remote_copy(
            src_ref=blocks_ref.at[source],
            dst_ref=out_ref.at[source],
            send_sem=send_sems.at[source],
            recv_sem=recv_sems.at[source],
            device_id=(partner, source),
            device_id_type=pl.DeviceIdType.MESH,
        ).wait_recv()
        return carry

    lax.fori_loop(0, n, finish, 0)


def partner_transpose(own_rows, vir_axis):
    n = lax.axis_size(vir_axis)
    rows, width = own_rows.shape
    blocks = jnp.transpose(own_rows.reshape(rows, n, width // n), (1, 2, 0))
    arrived = pl.pallas_call(
        functools.partial(_turn_kernel, n),
        out_shape=jax.ShapeDtypeStruct(blocks.shape, blocks.dtype),
        in_specs=[pl.BlockSpec(memory_space=pl.ANY)],
        out_specs=pl.BlockSpec(memory_space=pl.ANY),
        scratch_shapes=[pltpu.SemaphoreType.DMA((n,)), pltpu.SemaphoreType.DMA((n,))],
        compiler_params=pltpu.CompilerParams(collective_id=1, has_side_effects=True),
    )(blocks)
    return jnp.transpose(arrived, (1, 0, 2)).reshape(width // n, n * rows)


def per_device(amplitudes, factors, occ_energy, vir_energy, occ_irrep, vir_irrep, pair_orbitals):
    local_pairs = amplitudes.shape[0]
    row_count = amplitudes.shape[1]
    occ_total = occ_energy.shape[0]
    occ_devices = lax.axis_size("occ")
    vir_devices = lax.axis_size("vir")
    occ_index = lax.axis_index("occ")
    vir_index = lax.axis_index("vir")
    lower_half = occ_index < occ_devices // 2

    own = jnp.where(lower_half, amplitudes[0], amplitudes[1])
    outgoing = jnp.where(lower_half, amplitudes[1], amplitudes[0])
    other = passed_along(outgoing, "occ", occ_devices // 2)
    own, other = lax.optimization_barrier((own, other))

    def gather_rows(block):
        spread = jnp.broadcast_to(block[None], (vir_devices,) + block.shape)
        pieces = lax.all_to_all(spread, "vir", split_axis=0, concat_axis=0, tiled=True)
        return pieces.reshape(vir_devices * row_count, block.shape[-1])

    def half_products(rows):
        product = jnp.einsum("cd,qbd->qbc", rows, factors, preferred_element_type=jnp.float32)
        return product.astype(jnp.bfloat16)

    halves_first = half_products(gather_rows(own))
    direct = jnp.einsum("qac,qbc->ab", factors, halves_first, preferred_element_type=jnp.float32)
    own_rows = turned_rows(factors, gather_rows(other), direct, "vir")
    partner_cols = partner_transpose(own_rows, "vir")
    first_out = jnp.where(lower_half, own_rows, partner_cols)
    second_out = jnp.where(lower_half, partner_cols, own_rows)
    summed_pair = jnp.stack([first_out, second_out], axis=0)

    pair_ids = lax.dynamic_slice_in_dim(pair_orbitals, occ_index * local_pairs, local_pairs, 0)
    row_start = vir_index * row_count
    energy_rows = lax.dynamic_slice_in_dim(vir_energy, row_start, row_count, 0)
    irrep_rows = lax.dynamic_slice_in_dim(vir_irrep, row_start, row_count, 0)
    positions = jnp.arange(occ_total, dtype=jnp.int32)
    first_hot = positions[None, :] == pair_ids[:, 0:1]
    second_hot = positions[None, :] == pair_ids[:, 1:2]
    pair_energy = jnp.sum(jnp.where(first_hot, occ_energy[None, :], 0.0), axis=1) + jnp.sum(
        jnp.where(second_hot, occ_energy[None, :], 0.0), axis=1
    )
    first_irrep = jnp.sum(jnp.where(first_hot, occ_irrep[None, :], 0), axis=1)
    second_irrep = jnp.sum(jnp.where(second_hot, occ_irrep[None, :], 0), axis=1)
    pair_sym = jnp.bitwise_xor(first_irrep, second_irrep)
    combined_sym = jnp.bitwise_xor(
        jnp.bitwise_xor(pair_sym[:, None, None], irrep_rows[None, :, None]),
        vir_irrep[None, None, :],
    )
    allowed = combined_sym == 0
    denominator = (
        energy_rows[None, :, None] + vir_energy[None, None, :] - pair_energy[:, None, None]
    )
    return jnp.where(allowed, summed_pair / denominator, jnp.float32(0.0))


def solution(mesh):
    return jax.shard_map(
        per_device,
        mesh=mesh,
        in_specs=(P("occ", "vir", None), P("vir", None, None), P(), P(), P(), P(), P()),
        out_specs=P("occ", "vir", None),
        check_vma=False,
    )
```

```python
import functools

import jax
import jax.numpy as jnp
from jax import lax
from jax.sharding import PartitionSpec as P
from jax.experimental import pallas as pl
from jax.experimental.pallas import tpu as pltpu


def passed_along(block, axis, distance):
    devices = range(lax.axis_size(axis))
    route = [((i - distance) % len(devices), i) for i in devices]
    return lax.ppermute(block, axis, route)


def _turn_kernel(n, blocks_ref, out_ref, send_sems, recv_sems):
    me = lax.axis_index("vir")
    group = lax.axis_index("occ")
    partner = lax.rem(group + lax.axis_size("occ") // 2, lax.axis_size("occ"))

    barrier = pltpu.get_barrier_semaphore()

    def greet(k, carry):
        pl.semaphore_signal(barrier, inc=1, device_id=(partner, k), device_id_type=pl.DeviceIdType.MESH)
        return carry

    lax.fori_loop(0, n, greet, 0)
    pl.semaphore_wait(barrier, n)

    def copy_to(k):
        dest = lax.rem(me + k, n)
        return pltpu.make_async_remote_copy(
            src_ref=blocks_ref.at[dest],
            dst_ref=out_ref.at[me],
            send_sem=send_sems.at[dest],
            recv_sem=recv_sems.at[me],
            device_id=(partner, dest),
            device_id_type=pl.DeviceIdType.MESH,
        )

    def send(k, carry):
        copy_to(k).start()
        return carry

    lax.fori_loop(0, n, send, 0)

    def finish(k, carry):
        copy_to(k).wait_send()
        source = lax.rem(me + n - k, n)
        pltpu.make_async_remote_copy(
            src_ref=blocks_ref.at[source],
            dst_ref=out_ref.at[source],
            send_sem=send_sems.at[source],
            recv_sem=recv_sems.at[source],
            device_id=(partner, source),
            device_id_type=pl.DeviceIdType.MESH,
        ).wait_recv()
        return carry

    lax.fori_loop(0, n, finish, 0)


def partner_transpose(own_rows, vir_axis):
    n = lax.axis_size(vir_axis)
    rows, width = own_rows.shape
    blocks = jnp.transpose(own_rows.reshape(rows, n, width // n), (1, 2, 0))
    arrived = pl.pallas_call(
        functools.partial(_turn_kernel, n),
        out_shape=jax.ShapeDtypeStruct(blocks.shape, blocks.dtype),
        in_specs=[pl.BlockSpec(memory_space=pl.ANY)],
        out_specs=pl.BlockSpec(memory_space=pl.ANY),
        scratch_shapes=[pltpu.SemaphoreType.DMA((n,)), pltpu.SemaphoreType.DMA((n,))],
        compiler_params=pltpu.CompilerParams(collective_id=1, has_side_effects=True),
    )(blocks)
    return jnp.transpose(arrived, (1, 0, 2)).reshape(width // n, n * rows)


def per_device(amplitudes, factors, occ_energy, vir_energy, occ_irrep, vir_irrep, pair_orbitals):
    local_pairs = amplitudes.shape[0]
    row_count = amplitudes.shape[1]
    occ_total = occ_energy.shape[0]
    occ_devices = lax.axis_size("occ")
    vir_devices = lax.axis_size("vir")
    occ_index = lax.axis_index("occ")
    vir_index = lax.axis_index("vir")
    lower_half = occ_index < occ_devices // 2

    own = jnp.where(lower_half, amplitudes[0], amplitudes[1])
    outgoing = jnp.where(lower_half, amplitudes[1], amplitudes[0])
    spread_own = jnp.broadcast_to(own[None], (vir_devices,) + own.shape)
    other = passed_along(outgoing, "occ", occ_devices // 2)
    spread_other = jnp.broadcast_to(other[None], (vir_devices,) + other.shape)
    spread_own, spread_other = lax.optimization_barrier((spread_own, spread_other))

    def gather_rows(spread):
        pieces = lax.all_to_all(spread, "vir", split_axis=0, concat_axis=0, tiled=True)
        return pieces.reshape(vir_devices * row_count, spread.shape[-1])

    def half_products(rows):
        product = jnp.einsum("cd,qbd->qbc", rows, factors, preferred_element_type=jnp.float32)
        return product.astype(jnp.bfloat16)

    halves_first = half_products(gather_rows(spread_own))
    halves_second = half_products(gather_rows(spread_other))
    direct = jnp.einsum("qac,qbc->ab", factors, halves_first, preferred_element_type=jnp.float32)
    turned_term = jnp.einsum("qac,qbc->ab", halves_second, factors, preferred_element_type=jnp.float32)
    combined = direct + turned_term
    blocks = combined.reshape(vir_devices, row_count, combined.shape[-1]).astype(jnp.bfloat16)
    arrived = lax.all_to_all(blocks, "vir", split_axis=0, concat_axis=0, tiled=True)
    own_rows = jnp.sum(arrived.astype(jnp.float32), axis=0)
    partner_cols = partner_transpose(own_rows, "vir")
    first_out = jnp.where(lower_half, own_rows, partner_cols)
    second_out = jnp.where(lower_half, partner_cols, own_rows)
    summed_pair = jnp.stack([first_out, second_out], axis=0)

    pair_ids = lax.dynamic_slice_in_dim(pair_orbitals, occ_index * local_pairs, local_pairs, 0)
    row_start = vir_index * row_count
    energy_rows = lax.dynamic_slice_in_dim(vir_energy, row_start, row_count, 0)
    irrep_rows = lax.dynamic_slice_in_dim(vir_irrep, row_start, row_count, 0)
    positions = jnp.arange(occ_total, dtype=jnp.int32)
    first_hot = positions[None, :] == pair_ids[:, 0:1]
    second_hot = positions[None, :] == pair_ids[:, 1:2]
    pair_energy = jnp.sum(jnp.where(first_hot, occ_energy[None, :], 0.0), axis=1) + jnp.sum(
        jnp.where(second_hot, occ_energy[None, :], 0.0), axis=1
    )
    first_irrep = jnp.sum(jnp.where(first_hot, occ_irrep[None, :], 0), axis=1)
    second_irrep = jnp.sum(jnp.where(second_hot, occ_irrep[None, :], 0), axis=1)
    pair_sym = jnp.bitwise_xor(first_irrep, second_irrep)
    combined_sym = jnp.bitwise_xor(
        jnp.bitwise_xor(pair_sym[:, None, None], irrep_rows[None, :, None]),
        vir_irrep[None, None, :],
    )
    allowed = combined_sym == 0
    denominator = (
        energy_rows[None, :, None] + vir_energy[None, None, :] - pair_energy[:, None, None]
    )
    return jnp.where(allowed, summed_pair / denominator, jnp.float32(0.0))


def solution(mesh):
    return jax.shard_map(
        per_device,
        mesh=mesh,
        in_specs=(P("occ", "vir", None), P("vir", None, None), P(), P(), P(), P(), P()),
        out_specs=P("occ", "vir", None),
        check_vma=False,
    )
```

```python
import functools

import jax
import jax.numpy as jnp
from jax import lax
from jax.sharding import PartitionSpec as P
from jax.experimental import pallas as pl
from jax.experimental.pallas import tpu as pltpu


def passed_along(block, axis, distance):
    devices = range(lax.axis_size(axis))
    route = [((i - distance) % len(devices), i) for i in devices]
    return lax.ppermute(block, axis, route)


def _swap_kernel(amps_ref, own_ref, other_ref, sems):
    group = lax.axis_index("occ")
    me = lax.axis_index("vir")
    half = lax.axis_size("occ") // 2
    partner = lax.rem(group + half, lax.axis_size("occ"))
    upper = group // half
    send_sem, recv_sem, local_sem = sems

    barrier = pltpu.get_barrier_semaphore()
    pl.semaphore_signal(barrier, inc=1, device_id=(partner, me), device_id_type=pl.DeviceIdType.MESH)
    pl.semaphore_wait(barrier, 1)

    local = pltpu.make_async_copy(amps_ref.at[upper], own_ref, local_sem)
    local.start()
    trade = pltpu.make_async_remote_copy(
        src_ref=amps_ref.at[1 - upper],
        dst_ref=other_ref,
        send_sem=send_sem,
        recv_sem=recv_sem,
        device_id=(partner, me),
        device_id_type=pl.DeviceIdType.MESH,
    )
    trade.start()
    trade.wait()
    local.wait()


def swap_pairs(amplitudes):
    block = jax.ShapeDtypeStruct(amplitudes.shape[1:], amplitudes.dtype)
    return pl.pallas_call(
        _swap_kernel,
        out_shape=(block, block),
        in_specs=[pl.BlockSpec(memory_space=pl.ANY)],
        out_specs=(pl.BlockSpec(memory_space=pl.ANY), pl.BlockSpec(memory_space=pl.ANY)),
        scratch_shapes=[(pltpu.SemaphoreType.DMA, pltpu.SemaphoreType.DMA, pltpu.SemaphoreType.DMA)],
        compiler_params=pltpu.CompilerParams(collective_id=2, has_side_effects=True),
    )(amplitudes)


def _turn_kernel(n, blocks_ref, out_ref, send_sems, recv_sems):
    me = lax.axis_index("vir")
    group = lax.axis_index("occ")
    partner = lax.rem(group + lax.axis_size("occ") // 2, lax.axis_size("occ"))

    barrier = pltpu.get_barrier_semaphore()

    def greet(k, carry):
        pl.semaphore_signal(barrier, inc=1, device_id=(partner, k), device_id_type=pl.DeviceIdType.MESH)
        return carry

    lax.fori_loop(0, n, greet, 0)
    pl.semaphore_wait(barrier, n)

    def copy_to(k):
        dest = lax.rem(me + k, n)
        return pltpu.make_async_remote_copy(
            src_ref=blocks_ref.at[dest],
            dst_ref=out_ref.at[me],
            send_sem=send_sems.at[dest],
            recv_sem=recv_sems.at[me],
            device_id=(partner, dest),
            device_id_type=pl.DeviceIdType.MESH,
        )

    def send(k, carry):
        copy_to(k).start()
        return carry

    lax.fori_loop(0, n, send, 0)

    def finish(k, carry):
        copy_to(k).wait_send()
        source = lax.rem(me + n - k, n)
        pltpu.make_async_remote_copy(
            src_ref=blocks_ref.at[source],
            dst_ref=out_ref.at[source],
            send_sem=send_sems.at[source],
            recv_sem=recv_sems.at[source],
            device_id=(partner, source),
            device_id_type=pl.DeviceIdType.MESH,
        ).wait_recv()
        return carry

    lax.fori_loop(0, n, finish, 0)


def partner_transpose(own_rows, vir_axis):
    n = lax.axis_size(vir_axis)
    rows, width = own_rows.shape
    blocks = jnp.transpose(own_rows.reshape(rows, n, width // n), (1, 2, 0))
    arrived = pl.pallas_call(
        functools.partial(_turn_kernel, n),
        out_shape=jax.ShapeDtypeStruct(blocks.shape, blocks.dtype),
        in_specs=[pl.BlockSpec(memory_space=pl.ANY)],
        out_specs=pl.BlockSpec(memory_space=pl.ANY),
        scratch_shapes=[pltpu.SemaphoreType.DMA((n,)), pltpu.SemaphoreType.DMA((n,))],
        compiler_params=pltpu.CompilerParams(collective_id=1, has_side_effects=True),
    )(blocks)
    return jnp.transpose(arrived, (1, 0, 2)).reshape(width // n, n * rows)


def per_device(amplitudes, factors, occ_energy, vir_energy, occ_irrep, vir_irrep, pair_orbitals):
    local_pairs = amplitudes.shape[0]
    row_count = amplitudes.shape[1]
    occ_total = occ_energy.shape[0]
    occ_devices = lax.axis_size("occ")
    vir_devices = lax.axis_size("vir")
    occ_index = lax.axis_index("occ")
    vir_index = lax.axis_index("vir")
    lower_half = occ_index < occ_devices // 2

    own, other = swap_pairs(amplitudes)

    def gather_rows(block):
        spread = jnp.broadcast_to(block[None], (vir_devices,) + block.shape)
        pieces = lax.all_to_all(spread, "vir", split_axis=0, concat_axis=0, tiled=True)
        return pieces.reshape(vir_devices * row_count, block.shape[-1])

    def half_products(rows):
        product = jnp.einsum("cd,qbd->qbc", rows, factors, preferred_element_type=jnp.float32)
        return product.astype(jnp.bfloat16)

    halves_first = half_products(gather_rows(own))
    halves_second = half_products(gather_rows(other))
    direct = jnp.einsum("qac,qbc->ab", factors, halves_first, preferred_element_type=jnp.float32)
    turned_term = jnp.einsum("qac,qbc->ab", halves_second, factors, preferred_element_type=jnp.float32)
    combined = direct + turned_term
    blocks = combined.reshape(vir_devices, row_count, combined.shape[-1]).astype(jnp.bfloat16)
    arrived = lax.all_to_all(blocks, "vir", split_axis=0, concat_axis=0, tiled=True)
    own_rows = jnp.sum(arrived.astype(jnp.float32), axis=0)
    partner_cols = partner_transpose(own_rows, "vir")
    first_out = jnp.where(lower_half, own_rows, partner_cols)
    second_out = jnp.where(lower_half, partner_cols, own_rows)
    summed_pair = jnp.stack([first_out, second_out], axis=0)

    pair_ids = lax.dynamic_slice_in_dim(pair_orbitals, occ_index * local_pairs, local_pairs, 0)
    row_start = vir_index * row_count
    energy_rows = lax.dynamic_slice_in_dim(vir_energy, row_start, row_count, 0)
    irrep_rows = lax.dynamic_slice_in_dim(vir_irrep, row_start, row_count, 0)
    positions = jnp.arange(occ_total, dtype=jnp.int32)
    first_hot = positions[None, :] == pair_ids[:, 0:1]
    second_hot = positions[None, :] == pair_ids[:, 1:2]
    pair_energy = jnp.sum(jnp.where(first_hot, occ_energy[None, :], 0.0), axis=1) + jnp.sum(
        jnp.where(second_hot, occ_energy[None, :], 0.0), axis=1
    )
    first_irrep = jnp.sum(jnp.where(first_hot, occ_irrep[None, :], 0), axis=1)
    second_irrep = jnp.sum(jnp.where(second_hot, occ_irrep[None, :], 0), axis=1)
    pair_sym = jnp.bitwise_xor(first_irrep, second_irrep)
    combined_sym = jnp.bitwise_xor(
        jnp.bitwise_xor(pair_sym[:, None, None], irrep_rows[None, :, None]),
        vir_irrep[None, None, :],
    )
    allowed = combined_sym == 0
    denominator = (
        energy_rows[None, :, None] + vir_energy[None, None, :] - pair_energy[:, None, None]
    )
    return jnp.where(allowed, summed_pair / denominator, jnp.float32(0.0))


def solution(mesh):
    return jax.shard_map(
        per_device,
        mesh=mesh,
        in_specs=(P("occ", "vir", None), P("vir", None, None), P(), P(), P(), P(), P()),
        out_specs=P("occ", "vir", None),
        check_vma=False,
    )
```

```python
import functools

import jax
import jax.numpy as jnp
from jax import lax
from jax.sharding import PartitionSpec as P
from jax.experimental import pallas as pl
from jax.experimental.pallas import tpu as pltpu


def passed_along(block, axis, distance):
    devices = range(lax.axis_size(axis))
    route = [((i - distance) % len(devices), i) for i in devices]
    return lax.ppermute(block, axis, route)


def _turn_kernel(n, blocks_ref, out_ref, send_sems, recv_sems):
    me = lax.axis_index("vir")
    group = lax.axis_index("occ")
    partner = lax.rem(group + lax.axis_size("occ") // 2, lax.axis_size("occ"))

    barrier = pltpu.get_barrier_semaphore()

    def greet(k, carry):
        pl.semaphore_signal(barrier, inc=1, device_id=(partner, k), device_id_type=pl.DeviceIdType.MESH)
        return carry

    lax.fori_loop(0, n, greet, 0)
    pl.semaphore_wait(barrier, n)

    def copy_to(k):
        dest = lax.rem(me + k, n)
        return pltpu.make_async_remote_copy(
            src_ref=blocks_ref.at[dest],
            dst_ref=out_ref.at[me],
            send_sem=send_sems.at[dest],
            recv_sem=recv_sems.at[me],
            device_id=(partner, dest),
            device_id_type=pl.DeviceIdType.MESH,
        )

    def send(k, carry):
        copy_to(k).start()
        return carry

    lax.fori_loop(0, n, send, 0)

    def finish(k, carry):
        copy_to(k).wait_send()
        source = lax.rem(me + n - k, n)
        pltpu.make_async_remote_copy(
            src_ref=blocks_ref.at[source],
            dst_ref=out_ref.at[source],
            send_sem=send_sems.at[source],
            recv_sem=recv_sems.at[source],
            device_id=(partner, source),
            device_id_type=pl.DeviceIdType.MESH,
        ).wait_recv()
        return carry

    lax.fori_loop(0, n, finish, 0)


def partner_transpose(own_rows, vir_axis):
    n = lax.axis_size(vir_axis)
    rows, width = own_rows.shape
    blocks = jnp.transpose(own_rows.reshape(rows, n, width // n), (1, 2, 0))
    arrived = pl.pallas_call(
        functools.partial(_turn_kernel, n),
        out_shape=jax.ShapeDtypeStruct(blocks.shape, blocks.dtype),
        in_specs=[pl.BlockSpec(memory_space=pl.ANY)],
        out_specs=pl.BlockSpec(memory_space=pl.ANY),
        scratch_shapes=[pltpu.SemaphoreType.DMA((n,)), pltpu.SemaphoreType.DMA((n,))],
        compiler_params=pltpu.CompilerParams(collective_id=1, has_side_effects=True),
    )(blocks)
    return jnp.transpose(arrived, (1, 0, 2)).reshape(width // n, n * rows)


def per_device(amplitudes, factors, occ_energy, vir_energy, occ_irrep, vir_irrep, pair_orbitals):
    local_pairs = amplitudes.shape[0]
    row_count = amplitudes.shape[1]
    occ_total = occ_energy.shape[0]
    occ_devices = lax.axis_size("occ")
    vir_devices = lax.axis_size("vir")
    occ_index = lax.axis_index("occ")
    vir_index = lax.axis_index("vir")
    lower_half = occ_index < occ_devices // 2

    own = jnp.where(lower_half, amplitudes[0], amplitudes[1])
    outgoing = jnp.where(lower_half, amplitudes[1], amplitudes[0])
    other = passed_along(outgoing, "occ", occ_devices // 2)
    own, other = lax.optimization_barrier((own, other))

    def gather_rows(block):
        spread = jnp.broadcast_to(block[None], (vir_devices,) + block.shape)
        pieces = lax.all_to_all(spread, "vir", split_axis=0, concat_axis=0, tiled=True)
        return pieces.reshape(vir_devices * row_count, block.shape[-1])

    def half_products(rows):
        product = jnp.einsum("cd,qbd->qbc", rows, factors, preferred_element_type=jnp.float32)
        return product.astype(jnp.bfloat16)

    halves_first = half_products(gather_rows(own))
    other_rows = gather_rows(other)
    halves_second = jnp.einsum("cd,qad->qca", other_rows, factors, preferred_element_type=jnp.float32)
    halves_second = halves_second.astype(jnp.bfloat16)
    direct = jnp.einsum("qac,qbc->ab", factors, halves_first, preferred_element_type=jnp.float32)
    turned_term = jnp.einsum("qca,qbc->ab", halves_second, factors, preferred_element_type=jnp.float32)
    combined = direct + turned_term
    blocks = combined.reshape(vir_devices, row_count, combined.shape[-1]).astype(jnp.bfloat16)
    arrived = lax.all_to_all(blocks, "vir", split_axis=0, concat_axis=0, tiled=True)
    own_rows = jnp.sum(arrived.astype(jnp.float32), axis=0)
    partner_cols = partner_transpose(own_rows, "vir")
    first_out = jnp.where(lower_half, own_rows, partner_cols)
    second_out = jnp.where(lower_half, partner_cols, own_rows)
    summed_pair = jnp.stack([first_out, second_out], axis=0)

    pair_ids = lax.dynamic_slice_in_dim(pair_orbitals, occ_index * local_pairs, local_pairs, 0)
    row_start = vir_index * row_count
    energy_rows = lax.dynamic_slice_in_dim(vir_energy, row_start, row_count, 0)
    irrep_rows = lax.dynamic_slice_in_dim(vir_irrep, row_start, row_count, 0)
    positions = jnp.arange(occ_total, dtype=jnp.int32)
    first_hot = positions[None, :] == pair_ids[:, 0:1]
    second_hot = positions[None, :] == pair_ids[:, 1:2]
    pair_energy = jnp.sum(jnp.where(first_hot, occ_energy[None, :], 0.0), axis=1) + jnp.sum(
        jnp.where(second_hot, occ_energy[None, :], 0.0), axis=1
    )
    first_irrep = jnp.sum(jnp.where(first_hot, occ_irrep[None, :], 0), axis=1)
    second_irrep = jnp.sum(jnp.where(second_hot, occ_irrep[None, :], 0), axis=1)
    pair_sym = jnp.bitwise_xor(first_irrep, second_irrep)
    combined_sym = jnp.bitwise_xor(
        jnp.bitwise_xor(pair_sym[:, None, None], irrep_rows[None, :, None]),
        vir_irrep[None, None, :],
    )
    allowed = combined_sym == 0
    denominator = (
        energy_rows[None, :, None] + vir_energy[None, None, :] - pair_energy[:, None, None]
    )
    return jnp.where(allowed, summed_pair / denominator, jnp.float32(0.0))


def solution(mesh):
    return jax.shard_map(
        per_device,
        mesh=mesh,
        in_specs=(P("occ", "vir", None), P("vir", None, None), P(), P(), P(), P(), P()),
        out_specs=P("occ", "vir", None),
        check_vma=False,
    )
```
